512 devices in a mesh: blk: 32 (over x, z_hi, core), col: 16 (over y, z_lo).
Axes of the slice: x: 4, y: 8, z: 8 (z_hi: 4, z_lo: 2; z = z_hi * 2 + z_lo), core: 2. Of those that a mesh axis runs over, the one named last changes fastest.
Arguments:
- samples: bfloat16 [8192, 768], P('blk'), may hold values from -3 to 3
- targets: float32 [8192, 256], P('blk'), may hold values from -6 to 6
- batch_index: int32 [4096], P('blk'), may hold values from 0 to 255
- centers: bfloat16 [65536, 768], P(('blk', 'col')), may hold values from -3 to 3
- weights: float32 [65536, 256], P(('blk', 'col')), may hold values from -6 to 6
- nystrom_index: int32 [1536], replicated, may hold values from 0 to 65535, as said below
- eigvecs: float32 [1536, 128], replicated, may hold values from -0.15625 to 0.15625
- coefficient: float32 [128], replicated, may hold values from 0.4 to 0.95
Outputs:
- residual: float32 [4096, 256], P(('blk', 'col'))
- new_weights: float32 [65536, 256], P(('blk', 'col'))
The draws below stay inside these ranges and needn't reach their ends.
Inputs may be any that keep to these rules, and one draw needn't show every extreme that they name: Batch row i is sample row (i // 128) * 256 + batch_index[i]. `nystrom_index`: 1536 distinct center rows.
All inputs are finite; a program needn't handle non-finite values.
Results may differ from the reference program's by a relative error of at most 0.0003.
The reference program's roundings to bfloat16 on the way (of `points`, `kernel`, `weights_low` and `resid_low`) count: a program that leaves them out, or rounds other values in their place, can miss the bound.
Values may be sent and summed in bfloat16 or wider, within the bound.
A program may use at most 64 MiB of HBM per device.

```python
import math
import jax
import jax.numpy as jnp
from jax import lax

D = 768
C = 256
CEN_DEV = 128
BLK_ROWS = 128
SAMP_DEV = 256
NYS = 1536
TOPQ = 128
BATCH = 4096
SAMPLES = 8192
CENTERS = 65536
N_BLK = 32
N_COL = 16


latent_rank = 16


def point_rows(key, count, salt_value):
    basis = jax.random.normal(jax.random.fold_in(key, 9001), (D, latent_rank), jnp.float32)
    key_latent = jax.random.fold_in(key, salt_value)
    key_noise = jax.random.fold_in(key, salt_value + 1)
    latent = jax.random.normal(key_latent, (count, latent_rank), jnp.float32)
    noise_part = 2.0 * jax.random.normal(key_noise, (count, D), jnp.float32)
    values = (jnp.dot(latent, basis.T, precision=lax.Precision.HIGHEST) + noise_part) / math.sqrt(D)
    return jnp.clip(values, -3.0, 3.0)


def draw_samples(key, part):
    return point_rows(key, SAMPLES, 11).astype(jnp.bfloat16)


def draw_centers(key, part):
    return point_rows(key, CENTERS, 23).astype(jnp.bfloat16)


def draw_nystrom_index(key, part):
    order = jax.random.permutation(jax.random.fold_in(key, 37), CENTERS)
    return order[:NYS].astype(jnp.int32)


def set_ends(drawn, key, least, largest):
    spot = [jax.random.randint(jax.random.fold_in(key, axis), (), 0, length) for axis, length in enumerate(drawn.shape)]
    widest = drawn.shape.index(max(drawn.shape))
    neighbour = spot[:widest] + [(spot[widest] + 1) % drawn.shape[widest]] + spot[widest + 1:]
    return drawn.at[tuple(spot)].set(least).at[tuple(neighbour)].set(largest)


def levels(stream_key, shape, shards, smallest, high):
    def one(dim, blocks):
        heights = jax.random.uniform(jax.random.fold_in(jax.random.fold_in(stream_key, 6), dim), (blocks,), jnp.float32, smallest / len(shards), high / len(shards))
        return jnp.repeat(jnp.exp(heights), shape[dim] // blocks).reshape((-1,) + (1,) * (len(shape) - dim - 1))

    loudness = one(*shards[0])
    for cut in shards[1:]:
        loudness = loudness * one(*cut)
    return loudness


def centred(stream_key, shape, scale, bound, cuts=(), kind=jnp.bfloat16):
    entries = jax.random.normal(stream_key, shape, jnp.float32) * scale
    if len(cuts) > 0:
        entries = levels(stream_key, shape, cuts, -0.22, 0.18) * entries
    return jnp.clip(entries, min=-bound, max=bound).astype(kind)


def setup_inputs(seed: int = 0) -> dict:
    seeds = jax.random.split(jax.random.key(seed), 9)
    samples = draw_samples(jax.random.fold_in(seeds[8], 71), 0)
    targets = centred(seeds[1], (SAMPLES, C), 1.0, 6.0, ((0, 32),), jnp.float32)
    batch_index = set_ends(jax.random.randint(seeds[2], (BATCH,), 0, SAMP_DEV), jax.random.fold_in(seeds[2], 1), 0, SAMP_DEV - 1).astype(jnp.int32)
    centers = draw_centers(jax.random.fold_in(seeds[8], 71), 0)
    weights = centred(seeds[4], (CENTERS, C), 1.0, 6.0, ((0, 512),), jnp.float32)
    nystrom_index = draw_nystrom_index(jax.random.fold_in(seeds[8], 71), 0)
    eigvecs = centred(seeds[6], (NYS, TOPQ), NYS ** -0.5, 0.15625, (), jnp.float32)
    coefficient = jnp.clip(jax.random.uniform(seeds[7], (TOPQ,), jnp.float32, 0.4, 0.95), 0.4, 0.95)
    return {"samples": samples, "targets": targets, "batch_index": batch_index, "centers": centers, "weights": weights, "nystrom_index": nystrom_index, "eigvecs": eigvecs, "coefficient": coefficient}


spread = 1.0
shift_sq = 1.0
step_size = 4.0

def kernel_rows(points, centers):
    point_sq = lax.optimization_barrier(jnp.sum(jnp.square(points.astype(jnp.float32)), axis=1, keepdims=True))
    center_sq = lax.optimization_barrier(jnp.sum(jnp.square(centers.astype(jnp.float32)), axis=1))
    cross = lax.dot_general(points, centers, (((1,), (1,)), ((), ())), preferred_element_type=jnp.float32)
    dist_sq = point_sq + center_sq[None, :] - 2.0 * cross
    return jnp.exp(-jnp.sqrt(dist_sq + shift_sq) / spread).astype(jnp.bfloat16)

def reference(samples, targets, batch_index, centers, weights, nystrom_index, eigvecs, coefficient):
    owner_block = jnp.arange(BATCH, dtype=jnp.int32) // BLK_ROWS
    sample_row = (owner_block * SAMP_DEV + batch_index).astype(jnp.int32)
    points = jnp.take(samples, sample_row, axis=0)
    wanted = jnp.take(targets, sample_row, axis=0)
    weights_low = weights.astype(jnp.bfloat16)
    per_block = CEN_DEV * N_COL
    center_blocks = centers.reshape(N_BLK, per_block, D)
    weight_blocks = weights_low.reshape(N_BLK, per_block, C)

    def add_block(running, blocks_pair):
        center_part, weight_part = blocks_pair
        kernel = kernel_rows(points, center_part)
        return (running + jnp.dot(kernel, weight_part, preferred_element_type=jnp.float32), None)
    initial = jnp.zeros((BATCH, C), jnp.float32)
    prediction, _ = lax.scan(add_block, initial, (center_blocks, weight_blocks))
    residual = prediction - wanted
    resid_low = residual.astype(jnp.bfloat16)

    def grad_block(center_part):
        kernel = kernel_rows(points, center_part)
        return lax.dot_general(kernel, resid_low, (((0,), (0,)), ((), ())), preferred_element_type=jnp.float32)
    gradient = lax.map(grad_block, center_blocks).reshape(CENTERS, C)
    highest = lax.Precision.HIGHEST
    picked = jnp.take(gradient, nystrom_index, axis=0)
    projected = lax.dot_general(eigvecs, picked, (((0,), (0,)), ((), ())), precision=highest)
    correction = jnp.dot(eigvecs, coefficient[:, None] * projected, precision=highest)
    adjusted = gradient.at[nystrom_index].add(-correction)
    return (residual, weights - step_size * adjusted)
```

```python
import jax
import jax.numpy as jnp
from jax import lax
from jax.experimental import pallas as pl
from jax.experimental.pallas import tpu as pltpu
from jax.sharding import PartitionSpec as P

MESH = pl.DeviceIdType.MESH
F32, BF16 = jnp.float32, jnp.bfloat16

shift_sq = 1.0
step_size = 4.0

NX, NY, NZ, NH = 4, 8, 8, 4
RUN = 8
ROWS = 128
CHUNKS = 4


def spot(x, y, z, core):
    return (x * 8 + (z // 2) * 2 + core, y * 2 + z % 2)


def send(src, dst, send_sem, recv_sem, where):
    return pltpu.make_async_remote_copy(
        src_ref=src, dst_ref=dst, send_sem=send_sem, recv_sem=recv_sem, device_id=where, device_id_type=MESH
    )


def split3(v):
    a = v.astype(BF16)
    rest = v - a.astype(F32)
    b = rest.astype(BF16)
    c = (rest - b.astype(F32)).astype(BF16)
    return a, b, c


def nt(a, b):
    return lax.dot_general(a, b, (((1,), (1,)), ((), ())), preferred_element_type=F32)


def body(
    samples, targets, idx_row, centers, weights, nys, eig, coef, out_res, out_w,
    samp, targ, idx_v, idx_s, nys_v, eig_v, coef_v, wts,
    pts, cw, e123, ecat, csq, kmat, part, rec1, red1, rec2, rall, mall, gpart, grec, gs, gx,
    ld, zs, zr, xs, xr, cs, cr, s1, r1, s2, r2, gs1, gr1, gs2, gr2, ds, dr, dxs, dxr,
):
    blk, col = lax.axis_index("blk"), lax.axis_index("col")
    x, h, core = blk // 8, (blk // 2) % 4, blk % 2
    y, low = col // 2, col % 2
    z = 2 * h + low
    other = 1 - core

    def at_y(k):
        return spot(x, (y + k) % NY, z, core)

    def at_z(k):
        return spot(x, y, (z + k) % NZ, core)

    def at_x(k):
        return spot((x + k) % NX, y, z, core)

    partner = spot(x, y, z, other)

    barrier = pltpu.get_barrier_semaphore()

    def greet(k, carry):
        pl.semaphore_signal(barrier, inc=1, device_id=at_y(k), device_id_type=MESH)
        pl.semaphore_signal(barrier, inc=1, device_id=at_z(k), device_id_type=MESH)
        return carry

    lax.fori_loop(1, 8, greet, 0)
    for k in (1, 2, 3):
        pl.semaphore_signal(barrier, inc=1, device_id=at_x(k), device_id_type=MESH)
    pl.semaphore_signal(barrier, inc=1, device_id=partner, device_id_type=MESH)

    mine = core * 4 + x
    loads = [
        pltpu.make_async_copy(idx_row, idx_v, ld.at[0]),
        pltpu.make_async_copy(samples, samp, ld.at[1]),
        pltpu.make_async_copy(centers, cw.at[mine, :, pl.ds(0, 768)], ld.at[2]),
        pltpu.make_async_copy(weights, wts, ld.at[3]),
        pltpu.make_async_copy(nys, nys_v, ld.at[4]),
        pltpu.make_async_copy(eig, eig_v, ld.at[5]),
        pltpu.make_async_copy(coef, coef_v, ld.at[6]),
        pltpu.make_async_copy(targets, targ, ld.at[7]),
        pltpu.make_async_copy(idx_row, idx_s, ld.at[8]),
    ]
    for copy in loads:
        copy.start()
    for copy in loads[:4]:
        copy.wait()

    chosen = jnp.where(lax.broadcasted_iota(jnp.int32, (256, ROWS), 0) == idx_v[...], 1.0, 0.0).astype(F32)
    own = jnp.dot(chosen.T.astype(BF16), samp[...], preferred_element_type=F32)
    own = own.reshape(NY, 2, RUN, 768)
    own = jnp.concatenate([own[:, 0].reshape(64, 768), own[:, 1].reshape(64, 768)], axis=0)
    pts[h] = own.astype(BF16)
    cw[mine, :, 768:] = wts[...].astype(BF16)

    pl.semaphore_wait(barrier, 18)

    outward = 2 * low - 1
    zo, zi = spot(x, y, (z + outward + NZ) % NZ, core), spot(x, y, (z - outward + NZ) % NZ, core)
    h_a = ((z + outward + NZ) % NZ) // 2
    h_b = ((z - 2 * outward + NZ) % NZ) // 2
    h_c = ((z + 3 * outward + NZ) % NZ) // 2
    step = ROWS // CHUNKS

    def zpiece(block, kind, i, where):
        piece = pts.at[block, pl.ds(i * step, step), :]
        return send(piece, piece, zs.at[kind, i], zr.at[kind, i], where)

    x_next, x_prev, x_far = (x + 1) % NX, (x + 3) % NX, (x + 2) % NX
    right, left = at_x(1), at_x(3)

    def half(block_x, part_no, sem, where):
        piece = cw.at[core * 4 + block_x, pl.ds(part_no * 64, 64), :]
        return send(piece, piece, xs.at[sem], xr.at[sem], where)

    def across(block_core, block_x, sem):
        piece = cw.at[block_core * 4 + block_x]
        return send(piece, piece, cs.at[sem], cr.at[sem], partner)

    for i in range(CHUNKS):
        zpiece(h, 0, i, zo).start()
    half(x, 0, 0, right).start()
    half(x, 1, 1, left).start()
    half(x, 1, 2, right).start()
    half(x, 0, 3, left).start()
    across(core, x, 0).start()

    for copy in loads[4:]:
        copy.wait()
    e1, e2, e3 = split3(eig_v[...])
    e123[:, 0:128] = e1
    e123[:, 128:256] = e2
    e123[:, 256:384] = e3

    def eig_rows(j, carry):
        owner = ((j % 4) * 8 + h * 2 + j // 4) * 16 + col
        place = lax.broadcasted_iota(jnp.int32, (ROWS, 1536), 0) + owner * ROWS
        hit = jnp.where(place == nys_v[...], 1.0, 0.0).astype(BF16)
        ecat[j] = jnp.dot(hit, e123[...], preferred_element_type=F32).astype(BF16)
        return carry

    def relay_a(i):
        zpiece(h_a, 0, i, zo).wait_recv()
        zpiece(h_a, 1, i, zi).start()

    def relay_b(i):
        zpiece(h_b, 1, i, zi).wait_recv()
        zpiece(h_b, 2, i, zo).start()

    relay_a(0)
    relay_a(1)
    half(x_prev, 0, 0, right).wait_recv()
    half(x_prev, 0, 4, right).start()
    half(x_next, 1, 1, left).wait_recv()
    half(x_next, 1, 5, left).start()
    relay_b(0)
    relay_a(2)
    relay_b(1)
    relay_a(3)
    relay_b(2)
    half(x_prev, 1, 2, right).wait_recv()
    across(core, x_prev, 1).start()
    half(x_next, 0, 3, left).wait_recv()
    across(core, x_next, 2).start()
    relay_b(3)
    lax.fori_loop(0, 8, eig_rows, 0)
    half(x_far, 0, 4, right).wait_recv()
    half(x_far, 1, 5, left).wait_recv()
    across(core, x_far, 3).start()
    for i in range(CHUNKS):
        zpiece(h_c, 2, i, zo).wait_recv()
    across(other, x, 0).wait_recv()
    across(other, x_prev, 1).wait_recv()
    across(other, x_next, 2).wait_recv()
    across(other, x_far, 3).wait_recv()

    def norms(j, carry):
        c = cw[j, :, 0:768].astype(F32)
        total = jnp.sum(c * c, axis=1, keepdims=True)
        csq[j] = jnp.broadcast_to(total, (ROWS, ROWS)).T[0:8, :]
        return carry

    lax.fori_loop(0, 8, norms, 0)

    def tile(t, carry):
        p = pts[t]
        p32 = p.astype(F32)
        psq = jnp.sum(p32 * p32, axis=1, keepdims=True)
        for half_no in range(2):
            cen = cw[half_no * 4:half_no * 4 + 4, :, 0:768].reshape(512, 768)
            cross = nt(p, cen)
            row = jnp.concatenate([csq[half_no * 4 + i, 0:1, :] for i in range(4)], axis=1)
            dist = psq + row - 2.0 * cross
            kmat[t, :, half_no * 512:half_no * 512 + 512] = jnp.exp(-jnp.sqrt(dist + shift_sq)).astype(BF16)
        k = kmat[t]
        pred = jnp.dot(k, cw[:, :, 768:].reshape(1024, 256), preferred_element_type=F32)
        m = jnp.dot(k, ecat[...].reshape(1024, 384), preferred_element_type=F32)
        m = m[:, 0:128] + m[:, 128:256] + m[:, 256:384]
        rows = pl.ds(2 * t, 2)
        part[0, rows] = pred[:, 0:128].reshape(2, 8, RUN, 128)
        part[1, rows] = pred[:, 128:256].reshape(2, 8, RUN, 128)
        part[2, rows] = m.reshape(2, 8, RUN, 128)
        return carry

    lax.fori_loop(0, NH, tile, 0)

    def first(stream, k):
        if stream == 0:
            return send(part.at[0, :, (y + k) % NY], rec1.at[0, k], s1.at[0, k], r1.at[0, k], at_y(k))
        return send(part.at[stream, (z + k) % NZ], rec1.at[stream, k], s1.at[stream, k], r1.at[stream, k], at_z(k))

    def second(stream, k):
        if stream == 0:
            return send(red1.at[0, (z + k) % NZ], rec2.at[0, k], s2.at[0, k], r2.at[0, k], at_z(k))
        return send(red1.at[stream, (y + k) % NY], rec2.at[stream, k], s2.at[stream, k], r2.at[stream, k], at_y(k))

    def start_first(k, carry):
        for stream in range(3):
            first(stream, k).start()
        return carry

    lax.fori_loop(1, 8, start_first, 0)

    def finish_first(stream):
        own = part[0, :, y] if stream == 0 else part[stream, z]
        red1[stream] = own

        def add(k, carry):
            first(stream, k).wait_recv()
            red1[stream] += rec1[stream, k]
            return carry

        lax.fori_loop(1, 8, add, 0)

        def go(k, carry):
            second(stream, k).start()
            return carry

        lax.fori_loop(1, 8, go, 0)

    def finish_second(stream):
        def add(k, total):
            second(stream, k).wait_recv()
            return total + rec2[stream, k]

        return lax.fori_loop(1, 8, add, red1[stream, z if stream == 0 else y])

    finish_first(0)
    finish_first(1)
    finish_first(2)
    lo = finish_second(0)
    hi = finish_second(1)

    for r in range(RUN):
        row = idx_s[0, col * RUN + r]
        out_res[r:r + 1, :] = targ[pl.ds(row, 1), :]
    out_res[:, 0:128] = lo - out_res[:, 0:128]
    out_res[:, 128:256] = hi - out_res[:, 128:256]
    rall[z, y] = out_res[...].astype(BF16)

    def r_first(k, src_y):
        return send(rall.at[z, src_y], rall.at[z, src_y], gs1.at[0, k], gr1.at[0, k], at_y(k))

    def r_second(k, src_z):
        return send(rall.at[src_z], rall.at[src_z], gs2.at[0, k], gr2.at[0, k], at_z(k))

    def m_first(k, src_z):
        return send(mall.at[src_z, y], mall.at[src_z, y], gs1.at[1, k], gr1.at[1, k], at_z(k))

    def m_second(k, src_y):
        return send(mall.at[:, src_y], mall.at[:, src_y], gs2.at[1, k], gr2.at[1, k], at_y(k))

    def loop8(fn):
        def run(k, carry):
            fn(k)
            return carry

        lax.fori_loop(1, 8, run, 0)

    loop8(lambda k: r_first(k, y).start())
    mall[z, y] = finish_second(2)
    loop8(lambda k: m_first(k, z).start())
    loop8(lambda k: r_first(k, (y - k + NY) % NY).wait_recv())
    loop8(lambda k: r_second(k, z).start())
    loop8(lambda k: m_first(k, (z - k + NZ) % NZ).wait_recv())
    loop8(lambda k: m_second(k, y).start())
    loop8(lambda k: r_second(k, (z - k + NZ) % NZ).wait_recv())
    loop8(lambda k: m_second(k, (y - k + NY) % NY).wait_recv())

    resid = rall[...].astype(F32).reshape(512, 256)
    resid_t = resid.T.astype(BF16)
    m1, m2, m3 = split3(mall[...].reshape(512, 128))
    proj = (
        jnp.dot(resid_t, m1, preferred_element_type=F32)
        + jnp.dot(resid_t, m2, preferred_element_type=F32)
        + jnp.dot(resid_t, m3, preferred_element_type=F32)
    )
    a1, a2, a3 = split3(proj * coef_v[...])
    a_one = jnp.concatenate([a1, a1, a1], axis=1)
    a_two = jnp.concatenate([a2, a2], axis=1)

    def grad(i, carry):
        j = 4 * jnp.where(i < 4, other, core) + i % 4
        rows = pl.ds(pl.multiple_of(j * ROWS, ROWS), ROWS)
        km = kmat[:, :, rows].reshape(512, ROWS)
        e = ecat[j]
        g = jnp.dot(resid_t, km, preferred_element_type=F32)
        g = g - (nt(a_one, e) + nt(a_two, e[:, 0:256]) + nt(a3, e[:, 0:128]))
        gpart[j] = g
        return carry

    def swap(i):
        return send(gpart.at[other * 4 + i], grec.at[i], ds.at[i], dr.at[i], partner)

    lax.fori_loop(0, 4, grad, 0)
    for i in range(4):
        swap(i).start()
    lax.fori_loop(4, 8, grad, 0)

    def to_x(k):
        return send(gs.at[(x + k) % NX], gx.at[k], dxs.at[k], dxr.at[k], at_x(k))

    for i in range(4):
        swap(i).wait_recv()
        gs[i] = gpart[core * 4 + i] + grec[i]
    for k in (2, 1, 3):
        to_x(k).start()
    total = gs[x]
    for k in (1, 3, 2):
        to_x(k).wait_recv()
        total = total + gx[k]
    out_w[...] = wts[...] - step_size * total.T

    for i in range(CHUNKS):
        zpiece(h, 0, i, zo).wait_send()
        zpiece(h_a, 1, i, zi).wait_send()
        zpiece(h_b, 2, i, zo).wait_send()
    for i in range(6):
        half(x, 0, i, right).wait_send()
    for i in range(4):
        across(core, x, i).wait_send()
        swap(i).wait_send()
    for k in (1, 2, 3):
        to_x(k).wait_send()

    def drain(k):
        for stream in range(3):
            first(stream, k).wait_send()
            second(stream, k).wait_send()
        r_first(k, y).wait_send()
        r_second(k, z).wait_send()
        m_first(k, z).wait_send()
        m_second(k, y).wait_send()

    loop8(drain)


def local(samples, targets, batch_index, centers, weights, nystrom_index, eigvecs, coefficient):
    dma = pltpu.SemaphoreType.DMA
    vm = pltpu.VMEM
    return pl.pallas_call(
        body,
        out_shape=(jax.ShapeDtypeStruct((RUN, 256), F32), jax.ShapeDtypeStruct((ROWS, 256), F32)),
        in_specs=[pl.BlockSpec(memory_space=pl.ANY)] * 8,
        out_specs=(pl.BlockSpec(memory_space=pltpu.VMEM), pl.BlockSpec(memory_space=pltpu.VMEM)),
        scratch_shapes=[
            vm((256, 768), BF16), vm((256, 256), F32), vm((1, 128), jnp.int32), pltpu.SMEM((1, 128), jnp.int32),
            vm((1, 1536), jnp.int32), vm((1536, 128), F32), vm((1, 128), F32), vm((ROWS, 256), F32),
            vm((NH, ROWS, 768), BF16), vm((8, ROWS, 1024), BF16), vm((1536, 384), BF16), vm((8, ROWS, 384), BF16),
            vm((8, 8, ROWS), F32), vm((NH, ROWS, 1024), BF16),
            vm((3, 8, 8, RUN, 128), F32), vm((3, 8, 8, RUN, 128), F32), vm((3, 8, RUN, 128), F32),
            vm((3, 8, RUN, 128), F32), vm((8, 8, RUN, 256), BF16), vm((8, 8, RUN, 128), F32),
            vm((8, 256, ROWS), F32), vm((4, 256, ROWS), F32), vm((4, 256, ROWS), F32), vm((4, 256, ROWS), F32),
            dma((9,)), dma((3, CHUNKS)), dma((3, CHUNKS)), dma((6,)), dma((6,)), dma((4,)), dma((4,)),
            dma((3, 8)), dma((3, 8)), dma((3, 8)), dma((3, 8)),
            dma((2, 8)), dma((2, 8)), dma((2, 8)), dma((2, 8)), dma((4,)), dma((4,)), dma((4,)), dma((4,)),
        ],
        compiler_params=pltpu.CompilerParams(collective_id=0, has_side_effects=True, vmem_limit_bytes=48 << 20),
        name="step",
    )(
        samples, targets, batch_index.reshape(1, 128), centers, weights, nystrom_index.reshape(1, 1536),
        eigvecs, coefficient.reshape(1, 128),
    )


def solution(mesh):
    in_specs = (
        P("blk", None),
        P("blk", None),
        P("blk"),
        P(("blk", "col"), None),
        P(("blk", "col"), None),
        P(),
        P(),
        P(),
    )
    out_specs = (P(("blk", "col"), None), P(("blk", "col"), None))
    return jax.shard_map(local, mesh=mesh, in_specs=in_specs, out_specs=out_specs, check_vma=False)
```

```python
import jax
import jax.numpy as jnp
from jax import lax
from jax.experimental import pallas as pl
from jax.experimental.pallas import tpu as pltpu
from jax.sharding import PartitionSpec as P

MESH = pl.DeviceIdType.MESH
F32, BF16 = jnp.float32, jnp.bfloat16

shift_sq = 1.0
step_size = 4.0

NX, NY, NZ, NH = 4, 8, 8, 4
RUN = 8
ROWS = 128
STAGE = 9


def spot(x, y, z, core):
    return (x * 8 + (z // 2) * 2 + core, y * 2 + z % 2)


def send(src, dst, sems, where):
    return pltpu.make_async_remote_copy(
        src_ref=src, dst_ref=dst, send_sem=sems[0], recv_sem=sems[1], device_id=where, device_id_type=MESH
    )


def split3(v):
    a = v.astype(BF16)
    rest = v - a.astype(F32)
    b = rest.astype(BF16)
    c = (rest - b.astype(F32)).astype(BF16)
    return a, b, c


def nt(a, b):
    return lax.dot_general(a, b, (((1,), (1,)), ((), ())), preferred_element_type=F32)


def dot(a, b):
    return jnp.dot(a, b, preferred_element_type=F32)


def body(
    samples, targets, index, centers, weights, nys, eig, coef, out_res, out_w,
    samp, targ, idx_v, idx_s, nys_v, eig_v, coef_v, wts, want,
    pts, cen, wlo, e123, ecat, psq, csq, kmat,
    part_p, part_m, rec1_p, rec1_m, red_p, red_m, rec2_p, rec2_m, rall, mall, gpart, grec, gs, gx,
    ld, zs, zr, ys, yr, xs, xr, cs, cr, s1, r1, s2, r2, gs1, gr1, gs2, gr2, ds, dr, dxs, dxr,
):
    blk, col = lax.axis_index("blk"), lax.axis_index("col")
    x, h, core = blk // 8, (blk // 2) % 4, blk % 2
    y, low = col // 2, col % 2
    z = 2 * h + low
    other = 1 - core

    def at_y(k):
        return spot(x, (y + k) % NY, z, core)

    def at_z(k):
        return spot(x, y, (z + k) % NZ, core)

    def at_x(k):
        return spot((x + k) % NX, y, z, core)

    partner = spot(x, y, z, other)

    def loop(n, fn, start=0):
        def run(k, carry):
            fn(k)
            return carry

        lax.fori_loop(start, n, run, 0)

    def peers(fn):
        loop(7, lambda i: fn(4 + (i + 1) // 2 * (1 - 2 * (i % 2))))

    barrier = pltpu.get_barrier_semaphore()

    def greet(where):
        pl.semaphore_signal(barrier, inc=1, device_id=where, device_id_type=MESH)

    peers(lambda k: greet(at_z(k)))
    peers(lambda k: greet(at_y(k)))
    for k in (2, 1, 3):
        greet(at_x(k))
    greet(partner)

    mine = 2 * x + core
    loads = [
        pltpu.make_async_copy(index, idx_v.at[0], ld.at[0]),
        pltpu.make_async_copy(samples, samp, ld.at[1]),
        pltpu.make_async_copy(centers, cen.at[mine], ld.at[2]),
        pltpu.make_async_copy(weights, wts, ld.at[3]),
        pltpu.make_async_copy(nys, nys_v.at[0], ld.at[4]),
        pltpu.make_async_copy(eig, eig_v, ld.at[5]),
        pltpu.make_async_copy(coef, coef_v.at[0], ld.at[6]),
        pltpu.make_async_copy(targets, targ, ld.at[7]),
        pltpu.make_async_copy(index, idx_s.at[0], ld.at[8]),
    ]
    for copy in loads:
        copy.start()
    for copy in loads[:2]:
        copy.wait()

    chosen = jnp.where(lax.broadcasted_iota(jnp.int32, (256, ROWS), 0) == idx_v[...], 1.0, 0.0).astype(F32)
    own = dot(chosen.T.astype(BF16), samp[...]).reshape(NY, 2, RUN, 768)
    own = jnp.concatenate([own[:, 0].reshape(64, 768), own[:, 1].reshape(64, 768)], axis=0)
    pts[h] = own.astype(BF16)

    pl.semaphore_wait(barrier, 18)
    if STAGE == 0:
        for copy in loads[2:]:
            copy.wait()
        return

    outward = 2 * low - 1
    zo, zi = spot(x, y, (z + outward + NZ) % NZ, core), spot(x, y, (z - outward + NZ) % NZ, core)
    h_a = ((z + outward + NZ) % NZ) // 2
    h_b = ((z - 2 * outward + NZ) % NZ) // 2
    h_c = ((z + 3 * outward + NZ) % NZ) // 2
    parity = y % 2
    y_to = (at_y(1), at_y(7))

    def zpiece(block, kind, i, where):
        piece = pts.at[block, pl.ds(pl.multiple_of(parity * 64 + i * 32, 32), 32), :]
        return send(piece, piece, (zs.at[kind, i], zr.at[kind, i]), where)

    def ypiece(block, kind, i, side):
        piece = pts.at[block, pl.ds(pl.multiple_of(side * 64 + i * 32, 32), 32), :]
        return send(piece, piece, (ys.at[kind, i], yr.at[kind, i]), y_to[i])

    x_next, x_prev, x_far = (x + 1) % NX, (x + 3) % NX, (x + 2) % NX
    right, left = at_x(1), at_x(3)

    def half(block_x, part_no, sem, where):
        piece = cen.at[2 * block_x + core, pl.ds(part_no * 64, 64), :]
        return send(piece, piece, (xs.at[sem], xr.at[sem]), where)

    def weight(block_x, sem, where):
        piece = wlo.at[2 * block_x + core]
        return send(piece, piece, (xs.at[sem], xr.at[sem]), where)

    def weight_half(block_x, part_no, sem, where):
        piece = wlo.at[2 * block_x + core, pl.ds(part_no * 64, 64), :]
        return send(piece, piece, (xs.at[sem], xr.at[sem]), where)

    def across(ref, block_core, block_x, sem):
        piece = ref.at[2 * block_x + block_core]
        return send(piece, piece, (cs.at[sem], cr.at[sem]), partner)

    for i in range(2):
        zpiece(h, 0, i, zo).start()
    loads[2].wait()
    half(x, 0, 0, right).start()
    half(x, 1, 1, left).start()
    half(x, 1, 2, right).start()
    half(x, 0, 3, left).start()
    across(cen, core, x, 0).start()

    for copy in loads[3:]:
        copy.wait()
    wlo[mine] = wts[...].astype(BF16)

    e1, e2, e3 = split3(eig_v[...])
    e123[:, 0:128] = e1
    e123[:, 128:256] = e2
    e123[:, 256:384] = e3

    def eig_rows(j):
        owner = ((j // 2) * 8 + h * 2 + j % 2) * 16 + col
        place = lax.broadcasted_iota(jnp.int32, (ROWS, 1536), 0) + owner * ROWS
        hit = jnp.where(place == nys_v[...], 1.0, 0.0).astype(BF16)
        ecat[j] = dot(hit, e123[...]).astype(BF16)

    def relay_a(i):
        zpiece(h_a, 0, i, zo).wait_recv()
        zpiece(h_a, 1, i, zi).start()
        ypiece(h_a, 0, i, parity).start()

    def relay_b(i):
        zpiece(h_b, 1, i, zi).wait_recv()
        zpiece(h_b, 2, i, zo).start()
        ypiece(h_b, 1, i, parity).start()

    def relay_c(i):
        zpiece(h_c, 2, i, zo).wait_recv()
        ypiece(h_c, 2, i, parity).start()

    def points_ready(t):
        p32 = pts[t].astype(F32)
        psq[t] = jnp.sum(p32 * p32, axis=1, keepdims=True)

    def from_y(block, kind):
        for i in range(2):
            ypiece(block, kind, i, 1 - parity).wait_recv()
        points_ready(block)

    def centers_ready(xp):
        for c in range(2):
            v = cen[2 * xp + c].astype(F32)
            total = jnp.sum(v * v, axis=1, keepdims=True)
            csq[xp, :, c * 128:(c + 1) * 128] = jnp.broadcast_to(total, (ROWS, ROWS)).T[0:8, :]

    def unit(t, xp):
        cross = nt(pts[t], cen[pl.ds(2 * xp, 2)].reshape(256, 768))
        dist = psq[t] + csq[xp, 0:1, :] - 2.0 * cross
        kmat[t, xp] = jnp.exp(-jnp.sqrt(dist + shift_sq)).astype(BF16)

    loop(4, eig_rows)
    relay_a(0)
    loop(6, eig_rows, 4)
    relay_a(1)
    half(x_prev, 0, 0, right).wait_recv()
    half(x_prev, 0, 4, right).start()
    half(x_next, 1, 1, left).wait_recv()
    half(x_next, 1, 5, left).start()
    loop(8, eig_rows, 6)
    relay_b(0)
    points_ready(h)
    across(cen, other, x, 0).wait_recv()
    centers_ready(x)
    relay_b(1)
    unit(h, x)
    half(x_prev, 1, 2, right).wait_recv()
    across(cen, core, x_prev, 1).start()
    half(x_next, 0, 3, left).wait_recv()
    across(cen, core, x_next, 2).start()
    weight(x, 6, right).start()
    weight(x, 7, left).start()
    across(wlo, core, x, 4).start()
    from_y(h_a, 0)
    unit(h_a, x)
    relay_c(0)
    across(cen, other, x_prev, 1).wait_recv()
    centers_ready(x_prev)
    across(cen, other, x_next, 2).wait_recv()
    centers_ready(x_next)
    unit(h, x_prev)
    unit(h, x_next)
    relay_c(1)
    half(x_far, 0, 4, right).wait_recv()
    half(x_far, 1, 5, left).wait_recv()
    across(cen, core, x_far, 3).start()
    weight(x_prev, 6, right).wait_recv()
    weight_half(x_prev, 0, 8, right).start()
    across(wlo, core, x_prev, 5).start()
    weight(x_next, 7, left).wait_recv()
    weight_half(x_next, 1, 9, left).start()
    across(wlo, core, x_next, 6).start()
    unit(h_a, x_prev)
    unit(h_a, x_next)
    from_y(h_b, 1)
    unit(h_b, x)
    unit(h_b, x_prev)
    unit(h_b, x_next)
    across(cen, other, x_far, 3).wait_recv()
    centers_ready(x_far)
    unit(h, x_far)
    unit(h_a, x_far)
    unit(h_b, x_far)
    weight_half(x_far, 0, 8, right).wait_recv()
    weight_half(x_far, 1, 9, left).wait_recv()
    across(wlo, core, x_far, 7).start()
    from_y(h_c, 2)
    unit(h_c, x)
    unit(h_c, x_prev)
    unit(h_c, x_next)
    unit(h_c, x_far)
    across(wlo, other, x, 4).wait_recv()
    across(wlo, other, x_prev, 5).wait_recv()
    across(wlo, other, x_next, 6).wait_recv()
    across(wlo, other, x_far, 7).wait_recv()

    def store(ref, by_z, t, value):
        if by_z:
            ref[pl.ds(2 * t, 2)] = value
        else:
            for i in range(2):
                ref[:, 2 * t + i] = value[i]

    def product(t):
        pred = jnp.zeros((ROWS, 256), F32)
        m = jnp.zeros((ROWS, 384), F32)
        for xp in range(NX):
            k = kmat[t, xp]
            pred += dot(k, wlo[2 * xp:2 * xp + 2].reshape(256, 256))
            m += dot(k, ecat[2 * xp:2 * xp + 2].reshape(256, 384))
        m = m[:, 0:128] + m[:, 128:256] + m[:, 256:384]
        pred, m = pred.reshape(2, 8, RUN, 256), m.reshape(2, 8, RUN, 128)

        @pl.when(core == 0)
        def _():
            store(part_p, False, t, pred)
            store(part_m, True, t, m)

        @pl.when(core == 1)
        def _():
            store(part_p, True, t, pred)
            store(part_m, False, t, m)

    loop(NH, product)

    pred_stream = (part_p, rec1_p, red_p, rec2_p, 0, core)
    m_stream = (part_m, rec1_m, red_m, rec2_m, 1, 1 - core)

    def axes(by_z):
        return y + by_z * (z - y), z + by_z * (y - z)

    def first(stream, k):
        part, rec1, _, _, no, by_z = stream
        where = spot(x, (y + (1 - by_z) * k) % NY, (z + by_z * k) % NZ, core)
        return send(part.at[(axes(by_z)[0] + k) % 8], rec1.at[k], (s1.at[no, k], r1.at[no, k]), where)

    def second(stream, k):
        _, _, red, rec2, no, by_z = stream
        where = spot(x, (y + by_z * k) % NY, (z + (1 - by_z) * k) % NZ, core)
        return send(red.at[(axes(by_z)[1] + k) % 8], rec2.at[k], (s2.at[no, k], r2.at[no, k]), where)

    def finish_first(stream):
        part, rec1, red, _, _, by_z = stream
        red[...] = part[axes(by_z)[0]]

        def add(k):
            first(stream, k).wait_recv()
            red[...] += rec1[k]

        loop(8, add, 1)
        peers(lambda k: second(stream, k).start())

    def finish_second(stream):
        _, _, red, rec2, _, by_z = stream

        def add(k, total):
            second(stream, k).wait_recv()
            return total + rec2[k]

        return lax.fori_loop(1, 8, add, red[axes(by_z)[1]])

    def r_first(k, src_y):
        return send(rall.at[z, src_y], rall.at[z, src_y], (gs1.at[0, k], gr1.at[0, k]), at_y(k))

    def r_second(k, src_z):
        return send(rall.at[src_z], rall.at[src_z], (gs2.at[0, k], gr2.at[0, k]), at_z(k))

    def m_first(k, src_z):
        return send(mall.at[src_z, y], mall.at[src_z, y], (gs1.at[1, k], gr1.at[1, k]), at_z(k))

    def m_second(k, src_y):
        return send(mall.at[:, src_y], mall.at[:, src_y], (gs2.at[1, k], gr2.at[1, k]), at_y(k))

    def swap(i):
        return send(gpart.at[i, other], grec.at[i], (ds.at[i], dr.at[i]), partner)

    def to_x(k):
        return send(gs.at[(x + k) % NX], gx.at[k], (dxs.at[k], dxr.at[k]), at_x(k))

    def drain(stage):
        if stage >= 1:
            for i in range(2):
                zpiece(h, 0, i, zo).wait_send()
                zpiece(h_a, 1, i, zi).wait_send()
                zpiece(h_b, 2, i, zo).wait_send()
                ypiece(h_a, 0, i, parity).wait_send()
                ypiece(h_b, 1, i, parity).wait_send()
                ypiece(h_c, 2, i, parity).wait_send()
            for i in range(6):
                half(x, 0, i, right).wait_send()
            for i in range(2):
                weight(x, 6 + i, right).wait_send()
                weight_half(x, 0, 8 + i, right).wait_send()
            for i in range(4):
                across(cen, core, x, i).wait_send()
                across(wlo, core, x, 4 + i).wait_send()
        if stage >= 3:
            for stream in (pred_stream, m_stream):
                loop(8, lambda k: first(stream, k).wait_send(), 1)
                loop(8, lambda k: second(stream, k).wait_send(), 1)
        if stage >= 4:
            loop(8, lambda k: r_first(k, y).wait_send(), 1)
            loop(8, lambda k: r_second(k, z).wait_send(), 1)
            loop(8, lambda k: m_first(k, z).wait_send(), 1)
            loop(8, lambda k: m_second(k, y).wait_send(), 1)
        if stage >= 5:
            for i in range(4):
                swap(i).wait_send()
            for k in (1, 2, 3):
                to_x(k).wait_send()

    if STAGE == 2:
        return drain(1)

    peers(lambda k: first(pred_stream, k).start())
    peers(lambda k: first(m_stream, k).start())
    for r in range(RUN):
        row = idx_s[0, col * RUN + r]
        want[r:r + 1, :] = targ[pl.ds(row, 1), :]
    finish_first(pred_stream)
    finish_first(m_stream)

    out_res[...] = finish_second(pred_stream) - want[...]
    rall[z, y] = out_res[...].astype(BF16)
    if STAGE == 3:
        finish_second(m_stream)
        return drain(3)

    peers(lambda k: r_first(k, y).start())
    mall[z, y] = finish_second(m_stream)
    peers(lambda k: m_first(k, z).start())
    loop(8, lambda k: r_first(k, (y - k + NY) % NY).wait_recv(), 1)
    peers(lambda k: r_second(k, z).start())
    loop(8, lambda k: m_first(k, (z - k + NZ) % NZ).wait_recv(), 1)
    peers(lambda k: m_second(k, y).start())
    loop(8, lambda k: r_second(k, (z - k + NZ) % NZ).wait_recv(), 1)
    loop(8, lambda k: m_second(k, (y - k + NY) % NY).wait_recv(), 1)
    if STAGE == 4:
        return drain(4)

    resid_t = rall[...].astype(F32).reshape(512, 256).T.astype(BF16)
    m1, m2, m3 = split3(mall[...].reshape(512, 128))
    proj = dot(resid_t, m1) + dot(resid_t, m2) + dot(resid_t, m3)
    a1, a2, a3 = split3(proj * coef_v[...])
    a_one = jnp.concatenate([a1, a1, a1], axis=1)
    a_two = jnp.concatenate([a2, a2], axis=1)

    def grad(xp):
        e = ecat[pl.ds(2 * xp, 2)].reshape(256, 384)
        g = dot(resid_t, kmat[:, xp].reshape(512, 256))
        g = g - (nt(a_one, e) + nt(a_two, e[:, 0:256]) + nt(a3, e[:, 0:128]))
        gpart[xp, 0] = g[:, 0:128]
        gpart[xp, 1] = g[:, 128:256]
        swap(xp).start()

    def summed(k):
        xp = (x + k) % NX
        swap(xp).wait_recv()
        gs[xp] = gpart[xp, core] + grec[xp]
        if k:
            to_x(k).start()

    grad(x_far)
    grad(x_next)
    summed(2)
    grad(x_prev)
    summed(1)
    grad(x)
    summed(3)
    summed(0)
    total = gs[x]
    for k in (1, 3, 2):
        to_x(k).wait_recv()
        total = total + gx[k]
    out_w[...] = wts[...] - step_size * total.T
    drain(5)


def local(samples, targets, batch_index, centers, weights, nystrom_index, eigvecs, coefficient):
    dma = pltpu.SemaphoreType.DMA
    vm = pltpu.VMEM
    return pl.pallas_call(
        body,
        out_shape=(jax.ShapeDtypeStruct((RUN, 256), F32), jax.ShapeDtypeStruct((ROWS, 256), F32)),
        in_specs=[pl.BlockSpec(memory_space=pl.ANY)] * 8,
        out_specs=(pl.BlockSpec(memory_space=pltpu.VMEM), pl.BlockSpec(memory_space=pltpu.VMEM)),
        scratch_shapes=[
            vm((256, 768), BF16), vm((256, 256), F32), vm((1, 128), jnp.int32), pltpu.SMEM((1, 128), jnp.int32),
            vm((1, 1536), jnp.int32), vm((1536, 128), F32), vm((1, 128), F32), vm((ROWS, 256), F32), vm((RUN, 256), F32),
            vm((NH, ROWS, 768), BF16), vm((8, ROWS, 768), BF16), vm((8, ROWS, 256), BF16),
            vm((1536, 384), BF16), vm((8, ROWS, 384), BF16),
            vm((NH, ROWS, 1), F32), vm((NX, 8, 256), F32), vm((NH, NX, ROWS, 256), BF16),
            vm((8, 8, RUN, 256), F32), vm((8, 8, RUN, 128), F32), vm((8, 8, RUN, 256), F32), vm((8, 8, RUN, 128), F32),
            vm((8, RUN, 256), F32), vm((8, RUN, 128), F32), vm((8, RUN, 256), F32), vm((8, RUN, 128), F32),
            vm((8, 8, RUN, 256), BF16), vm((8, 8, RUN, 128), F32),
            vm((NX, 2, 256, ROWS), F32), vm((NX, 256, ROWS), F32), vm((NX, 256, ROWS), F32), vm((NX, 256, ROWS), F32),
            dma((9,)), dma((3, 2)), dma((3, 2)), dma((3, 2)), dma((3, 2)), dma((10,)), dma((10,)), dma((8,)), dma((8,)),
            dma((2, 8)), dma((2, 8)), dma((2, 8)), dma((2, 8)),
            dma((2, 8)), dma((2, 8)), dma((2, 8)), dma((2, 8)), dma((4,)), dma((4,)), dma((4,)), dma((4,)),
        ],
        compiler_params=pltpu.CompilerParams(collective_id=0, has_side_effects=True, vmem_limit_bytes=67043328),
        name="step",
    )(samples, targets, batch_index, centers, weights, nystrom_index, eigvecs, coefficient)


def solution(mesh):
    in_specs = (
        P("blk", None),
        P("blk", None),
        P("blk"),
        P(("blk", "col"), None),
        P(("blk", "col"), None),
        P(),
        P(),
        P(),
    )
    out_specs = (P(("blk", "col"), None), P(("blk", "col"), None))
    return jax.shard_map(local, mesh=mesh, in_specs=in_specs, out_specs=out_specs, check_vma=False)
```

```python
import jax
import jax.numpy as jnp
from jax import lax
from jax.experimental import pallas as pl
from jax.experimental.pallas import tpu as pltpu
from jax.sharding import PartitionSpec as P

MESH = pl.DeviceIdType.MESH
F32, BF16 = jnp.float32, jnp.bfloat16

shift_sq = 1.0
step_size = 4.0

NX, NY, NZ, NH = 4, 8, 8, 4
RUN = 8
ROWS = 128
STAGE = 9


def spot(x, y, z, core):
    return (x * 8 + (z // 2) * 2 + core, y * 2 + z % 2)


def send(src, dst, sems, where):
    return pltpu.make_async_remote_copy(
        src_ref=src, dst_ref=dst, send_sem=sems[0], recv_sem=sems[1], device_id=where, device_id_type=MESH
    )


def split3(v):
    a = v.astype(BF16)
    rest = v - a.astype(F32)
    b = rest.astype(BF16)
    c = (rest - b.astype(F32)).astype(BF16)
    return a, b, c


def nt(a, b):
    return lax.dot_general(a, b, (((1,), (1,)), ((), ())), preferred_element_type=F32)


def dot(a, b):
    return jnp.dot(a, b, preferred_element_type=F32)


def body(
    samples, targets, index, centers, weights, nys, eig, coef, out_res, out_w,
    samp, targ, idx_v, idx_s, nys_v, eig_v, coef_v, wts, want,
    pts, cen, wlo, e123, ecat, psq, csq, kmat,
    part_p, part_m, rec1_p, rec1_m, red_p, red_m, rec2_p, rec2_m, rall, mall, gpart, grec, gs, gx,
    ld, zs, zr, ys, yr, xs, xr, cs, cr, s1, r1, s2, r2, gs1, gr1, gs2, gr2, ds, dr, dxs, dxr, near,
):
    blk, col = lax.axis_index("blk"), lax.axis_index("col")
    x, h, core = blk // 8, (blk // 2) % 4, blk % 2
    y, low = col // 2, col % 2
    z = 2 * h + low
    other = 1 - core

    def at_y(k):
        return spot(x, (y + k) % NY, z, core)

    def at_z(k):
        return spot(x, y, (z + k) % NZ, core)

    def at_x(k):
        return spot((x + k) % NX, y, z, core)

    partner = spot(x, y, z, other)

    def loop(n, fn, start=0):
        def run(k, carry):
            fn(k)
            return carry

        lax.fori_loop(start, n, run, 0)

    def peers(fn):
        loop(7, lambda i: fn(4 + (i + 1) // 2 * (1 - 2 * (i % 2))))

    barrier = pltpu.get_barrier_semaphore()

    def greet(where):
        pl.semaphore_signal(barrier, inc=1, device_id=where, device_id_type=MESH)

    for where in (at_z(1), at_z(7), at_y(1), at_y(7), at_x(1), at_x(3), partner):
        greet(where)

    mine = 2 * x + core
    loads = [
        pltpu.make_async_copy(index, idx_v.at[0], ld.at[0]),
        pltpu.make_async_copy(samples, samp, ld.at[1]),
        pltpu.make_async_copy(centers, cen.at[mine], ld.at[2]),
        pltpu.make_async_copy(weights, wts, ld.at[3]),
        pltpu.make_async_copy(nys, nys_v.at[0], ld.at[4]),
        pltpu.make_async_copy(eig, eig_v, ld.at[5]),
        pltpu.make_async_copy(coef, coef_v.at[0], ld.at[6]),
        pltpu.make_async_copy(targets, targ, ld.at[7]),
        pltpu.make_async_copy(index, idx_s.at[0], ld.at[8]),
    ]
    for copy in loads:
        copy.start()
    for copy in loads[:2]:
        copy.wait()

    chosen = jnp.where(lax.broadcasted_iota(jnp.int32, (256, ROWS), 0) == idx_v[...], 1.0, 0.0).astype(F32)
    own = dot(chosen.T.astype(BF16), samp[...]).reshape(NY, 2, RUN, 768)
    own = jnp.concatenate([own[:, 0].reshape(64, 768), own[:, 1].reshape(64, 768)], axis=0)
    pts[0] = own.astype(BF16)

    pl.semaphore_wait(barrier, 7)
    if STAGE == 0:
        for copy in loads[2:]:
            copy.wait()
        return

    outward = 2 * low - 1
    zo, zi = spot(x, y, (z + outward + NZ) % NZ, core), spot(x, y, (z - outward + NZ) % NZ, core)
    h_a = ((z + outward + NZ) % NZ) // 2
    h_b = ((z - 2 * outward + NZ) % NZ) // 2
    h_c = ((z + 3 * outward + NZ) % NZ) // 2
    parity = y % 2
    y_to = (at_y(1), at_y(7))

    def zpiece(kind, i, where):
        rows = pl.ds(pl.multiple_of(parity * 64 + i * 32, 32), 32)
        return send(pts.at[kind, rows, :], pts.at[kind + 1, rows, :], (zs.at[kind, i], zr.at[kind, i]), where)

    def ypiece(kind, i, side):
        piece = pts.at[kind + 1, pl.ds(pl.multiple_of(side * 64 + i * 32, 32), 32), :]
        return send(piece, piece, (ys.at[kind, i], yr.at[kind, i]), y_to[i])

    x_next, x_prev, x_far = (x + 1) % NX, (x + 3) % NX, (x + 2) % NX
    right, left = at_x(1), at_x(3)

    def half(block_x, part_no, sem, where):
        piece = cen.at[2 * block_x + core, pl.ds(part_no * 64, 64), :]
        return send(piece, piece, (xs.at[sem], xr.at[sem]), where)

    def weight(block_x, sem, where):
        piece = wlo.at[2 * block_x + core]
        return send(piece, piece, (xs.at[sem], xr.at[sem]), where)

    def weight_half(block_x, part_no, sem, where):
        piece = wlo.at[2 * block_x + core, pl.ds(part_no * 64, 64), :]
        return send(piece, piece, (xs.at[sem], xr.at[sem]), where)

    def across(ref, block_core, block_x, sem):
        piece = ref.at[2 * block_x + block_core]
        return send(piece, piece, (cs.at[sem], cr.at[sem]), partner)

    def hello(no, k):
        for where in (at_y(k), at_y(8 - k)):
            pl.semaphore_signal(near.at[no], inc=1, device_id=where, device_id_type=MESH)

    for i in range(2):
        zpiece(0, i, zo).start()
    hello(0, 1)
    loads[2].wait()
    half(x, 0, 0, right).start()
    half(x, 1, 1, left).start()
    half(x, 1, 2, right).start()
    half(x, 0, 3, left).start()
    across(cen, core, x, 0).start()

    for copy in loads[3:]:
        copy.wait()
    wlo[mine] = wts[...].astype(BF16)

    e1, e2, e3 = split3(eig_v[...])
    e123[:, 0:128] = e1
    e123[:, 128:256] = e2
    e123[:, 256:384] = e3

    def eig_rows(xp):
        owner = (xp * 8 + h * 2 + core) * 16 + col
        place = lax.broadcasted_iota(jnp.int32, (ROWS, 1536), 0) + owner * ROWS
        hit = jnp.where(place == nys_v[...], 1.0, 0.0).astype(BF16)
        ecat[2 * xp + core] = dot(hit, e123[...]).astype(BF16)

    def relay_a(i):
        zpiece(0, i, zo).wait_recv()
        zpiece(1, i, zi).start()
        ypiece(0, i, parity).start()

    def relay_b(i):
        zpiece(1, i, zi).wait_recv()
        zpiece(2, i, zo).start()
        ypiece(1, i, parity).start()

    def relay_c(i):
        zpiece(2, i, zo).wait_recv()
        ypiece(2, i, parity).start()

    def points_ready(slot):
        p32 = pts[slot].astype(F32)
        psq[slot] = jnp.sum(p32 * p32, axis=1, keepdims=True)

    def from_y(kind):
        for i in range(2):
            ypiece(kind, i, 1 - parity).wait_recv()
        points_ready(kind + 1)

    def centers_ready(xp):
        for c in range(2):
            v = cen[2 * xp + c].astype(F32)
            total = jnp.sum(v * v, axis=1, keepdims=True)
            csq[xp, :, c * 128:(c + 1) * 128] = jnp.broadcast_to(total, (ROWS, ROWS)).T[0:8, :]

    def pair(xp):
        return pl.ds(pl.multiple_of(xp * 256, 256), 256)

    def unit(slot, end, xp):
        rows = (end - slot) * ROWS
        cross = nt(pts[slot:end].reshape(rows, 768), cen[pl.ds(2 * xp, 2)].reshape(256, 768))
        shifted = psq[slot:end].reshape(rows, 1) + csq[xp, 0:1, :] - 2.0 * cross + shift_sq
        kmat[slot * ROWS:end * ROWS, pair(xp)] = jnp.exp(-(shifted * lax.rsqrt(shifted))).astype(BF16)

    loop(2, eig_rows)
    relay_a(0)
    pl.semaphore_wait(near.at[0], 2)
    hello(1, 2)
    loop(3, eig_rows, 2)
    relay_a(1)
    half(x_prev, 0, 0, right).wait_recv()
    half(x_prev, 0, 4, right).start()
    half(x_next, 1, 1, left).wait_recv()
    half(x_next, 1, 5, left).start()
    weight(x, 6, right).start()
    weight(x, 7, left).start()
    across(wlo, core, x, 4).start()
    loop(4, eig_rows, 3)
    for i in range(4):
        across(ecat, core, i, 8 + i).start()
    relay_b(0)
    points_ready(0)
    across(cen, other, x, 0).wait_recv()
    centers_ready(x)
    relay_b(1)
    half(x_prev, 1, 2, right).wait_recv()
    across(cen, core, x_prev, 1).start()
    half(x_next, 0, 3, left).wait_recv()
    across(cen, core, x_next, 2).start()
    from_y(0)
    unit(0, 2, x)
    relay_c(0)
    across(cen, other, x_prev, 1).wait_recv()
    centers_ready(x_prev)
    across(cen, other, x_next, 2).wait_recv()
    centers_ready(x_next)
    unit(0, 2, x_prev)
    weight(x_prev, 6, right).wait_recv()
    weight_half(x_prev, 0, 8, right).start()
    across(wlo, core, x_prev, 5).start()
    weight(x_next, 7, left).wait_recv()
    weight_half(x_next, 1, 9, left).start()
    across(wlo, core, x_next, 6).start()
    relay_c(1)
    half(x_far, 0, 4, right).wait_recv()
    half(x_far, 1, 5, left).wait_recv()
    across(cen, core, x_far, 3).start()
    unit(0, 2, x_next)
    from_y(1)
    across(cen, other, x_far, 3).wait_recv()
    centers_ready(x_far)
    unit(0, 3, x_far)
    from_y(2)
    unit(2, 4, x)
    weight_half(x_far, 0, 8, right).wait_recv()
    weight_half(x_far, 1, 9, left).wait_recv()
    across(wlo, core, x_far, 7).start()
    unit(2, 4, x_prev)
    unit(2, 4, x_next)
    unit(3, 4, x_far)
    for i, xp in enumerate((x, x_prev, x_next, x_far)):
        across(wlo, other, xp, 4 + i).wait_recv()
        across(ecat, other, i, 8 + i).wait_recv()
    pl.semaphore_wait(near.at[1], 2)

    def store(ref, by_z, t, value):
        if by_z:
            ref[pl.ds(2 * t, 2)] = value
        else:
            for i in range(2):
                ref[:, 2 * t + i] = value[i]

    pred = dot(kmat[...], wlo[...].reshape(1024, 256)).reshape(NH, 2, 8, RUN, 256)
    m = dot(kmat[...], ecat[...].reshape(1024, 384))
    m = (m[:, 0:128] + m[:, 128:256] + m[:, 256:384]).reshape(NH, 2, 8, RUN, 128)
    slots = (h, h_a, h_b, h_c)

    @pl.when(core == 0)
    def _():
        for i in range(NH):
            store(part_p, False, slots[i], pred[i])
            store(part_m, True, slots[i], m[i])

    @pl.when(core == 1)
    def _():
        for i in range(NH):
            store(part_p, True, slots[i], pred[i])
            store(part_m, False, slots[i], m[i])

    pred_stream = (part_p, rec1_p, red_p, rec2_p, 0, core)
    m_stream = (part_m, rec1_m, red_m, rec2_m, 1, 1 - core)

    def axes(by_z):
        return y + by_z * (z - y), z + by_z * (y - z)

    def first(stream, k):
        part, rec1, _, _, no, by_z = stream
        where = spot(x, (y + (1 - by_z) * k) % NY, (z + by_z * k) % NZ, core)
        return send(part.at[(axes(by_z)[0] + k) % 8], rec1.at[k], (s1.at[no, k], r1.at[no, k]), where)

    def second(stream, k):
        _, _, red, rec2, no, by_z = stream
        where = spot(x, (y + by_z * k) % NY, (z + (1 - by_z) * k) % NZ, core)
        return send(red.at[(axes(by_z)[1] + k) % 8], rec2.at[k], (s2.at[no, k], r2.at[no, k]), where)

    def finish_first(stream):
        part, rec1, red, _, _, by_z = stream
        red[...] = part[axes(by_z)[0]]

        def add(k):
            first(stream, k).wait_recv()
            red[...] += rec1[k]

        loop(8, add, 1)
        peers(lambda k: second(stream, k).start())

    def finish_second(stream):
        _, _, red, rec2, _, by_z = stream

        def add(k, total):
            second(stream, k).wait_recv()
            return total + rec2[k]

        return lax.fori_loop(1, 8, add, red[axes(by_z)[1]])

    def r_first(k, src_y):
        return send(rall.at[z, src_y], rall.at[z, src_y], (gs1.at[0, k], gr1.at[0, k]), at_y(k))

    def r_second(k, src_z):
        return send(rall.at[src_z], rall.at[src_z], (gs2.at[0, k], gr2.at[0, k]), at_z(k))

    def m_first(k, src_z):
        return send(mall.at[src_z, y], mall.at[src_z, y], (gs1.at[1, k], gr1.at[1, k]), at_z(k))

    def m_second(k, src_y):
        return send(mall.at[:, src_y], mall.at[:, src_y], (gs2.at[1, k], gr2.at[1, k]), at_y(k))

    def swap(i):
        return send(gpart.at[i, other], grec.at[i], (ds.at[i], dr.at[i]), partner)

    def top(ref):
        return ref.at[0:128]

    def bottom(ref):
        return ref.at[128:256]

    def far_half(i):
        part_of = (top, bottom)[i]
        return send(part_of(gs.at[x_far]), gx.at[2, pl.ds(128 * i, 128)], (dxs.at[i], dxr.at[i]), (right, left)[i])

    def near_half(side, i):
        part_of = (top, bottom)[i]
        block, where = (gs.at[x_next], right) if side == 0 else (gs.at[x_prev], left)
        sem = 2 + 2 * side + i
        return send(part_of(block), gx.at[side, pl.ds(128 * i, 128)], (dxs.at[sem], dxr.at[sem]), where)

    def drain(stage):
        if stage >= 1:
            for i in range(2):
                zpiece(0, i, zo).wait_send()
                zpiece(1, i, zi).wait_send()
                zpiece(2, i, zo).wait_send()
                for kind in range(3):
                    ypiece(kind, i, parity).wait_send()
            for i in range(6):
                half(x, 0, i, right).wait_send()
            for i in range(2):
                weight(x, 6 + i, right).wait_send()
                weight_half(x, 0, 8 + i, right).wait_send()
            for i in range(4):
                across(cen, core, x, i).wait_send()
                across(wlo, core, x, 4 + i).wait_send()
                across(ecat, core, x, 8 + i).wait_send()
        if stage >= 3:
            for stream in (pred_stream, m_stream):
                loop(8, lambda k: first(stream, k).wait_send(), 1)
                loop(8, lambda k: second(stream, k).wait_send(), 1)
        if stage >= 4:
            loop(8, lambda k: r_first(k, y).wait_send(), 1)
            loop(8, lambda k: r_second(k, z).wait_send(), 1)
            loop(8, lambda k: m_first(k, z).wait_send(), 1)
            loop(8, lambda k: m_second(k, y).wait_send(), 1)
        if stage >= 5:
            for i in range(4):
                swap(i).wait_send()
            for i in range(2):
                far_half(i).wait_send()
                near_half(0, i).wait_send()
                near_half(1, i).wait_send()

    if STAGE == 2:
        return drain(1)

    peers(lambda k: first(pred_stream, k).start())
    peers(lambda k: first(m_stream, k).start())
    for r in range(RUN):
        row = idx_s[0, col * RUN + r]
        want[r:r + 1, :] = targ[pl.ds(row, 1), :]
    finish_first(pred_stream)
    finish_first(m_stream)

    out_res[...] = finish_second(pred_stream) - want[...]
    rall[z, y] = out_res[...].astype(BF16)
    if STAGE == 3:
        finish_second(m_stream)
        return drain(3)

    peers(lambda k: r_first(k, y).start())
    mall[z, y] = finish_second(m_stream)
    peers(lambda k: m_first(k, z).start())
    loop(8, lambda k: r_first(k, (y - k + NY) % NY).wait_recv(), 1)
    peers(lambda k: r_second(k, z).start())
    loop(8, lambda k: m_first(k, (z - k + NZ) % NZ).wait_recv(), 1)
    peers(lambda k: m_second(k, y).start())
    loop(8, lambda k: r_second(k, (z - k + NZ) % NZ).wait_recv(), 1)
    loop(8, lambda k: m_second(k, (y - k + NY) % NY).wait_recv(), 1)
    if STAGE == 4:
        return drain(4)

    resid = jnp.concatenate([rall[pl.ds(2 * t, 2)].astype(F32).reshape(ROWS, 256) for t in slots], axis=0)
    resid_t = resid.T.astype(BF16)
    m_slots = jnp.concatenate([mall[pl.ds(2 * t, 2)].reshape(ROWS, 128) for t in slots], axis=0)
    m1, m2, m3 = split3(m_slots)
    proj = dot(resid_t, m1) + dot(resid_t, m2) + dot(resid_t, m3)
    a1, a2, a3 = split3(proj * coef_v[...])
    a_one = jnp.concatenate([a1, a1, a1], axis=1)
    a_two = jnp.concatenate([a2, a2], axis=1)

    def grad(xp):
        e = ecat[pl.ds(2 * xp, 2)].reshape(256, 384)
        g = dot(resid_t, kmat[:, pair(xp)])
        g = g - (nt(a_one, e) + nt(a_two, e[:, 0:256]) + nt(a3, e[:, 0:128]))
        gpart[xp, 0] = g[:, 0:128]
        gpart[xp, 1] = g[:, 128:256]
        swap(xp).start()

    def summed(xp):
        swap(xp).wait_recv()
        gs[xp] = gpart[xp, core] + grec[xp]

    grad(x_far)
    grad(x_next)
    summed(x_far)
    far_half(0).start()
    far_half(1).start()
    grad(x_prev)
    summed(x_next)
    near_half(0, 1).start()
    grad(x)
    summed(x_prev)
    near_half(1, 0).start()
    far_half(0).wait_recv()
    gs[x_next, 0:128, :] += gx[2, 0:128, :]
    near_half(0, 0).start()
    far_half(1).wait_recv()
    gs[x_prev, 128:256, :] += gx[2, 128:256, :]
    near_half(1, 1).start()
    summed(x)
    near_half(0, 1).wait_recv()
    near_half(1, 0).wait_recv()
    near_half(0, 0).wait_recv()
    near_half(1, 1).wait_recv()
    total = gs[x] + gx[0] + gx[1]
    out_w[...] = wts[...] - step_size * total.T
    drain(5)


def local(samples, targets, batch_index, centers, weights, nystrom_index, eigvecs, coefficient):
    dma = pltpu.SemaphoreType.DMA
    vm = pltpu.VMEM
    return pl.pallas_call(
        body,
        out_shape=(jax.ShapeDtypeStruct((RUN, 256), F32), jax.ShapeDtypeStruct((ROWS, 256), F32)),
        in_specs=[pl.BlockSpec(memory_space=pl.ANY)] * 8,
        out_specs=(pl.BlockSpec(memory_space=pltpu.VMEM), pl.BlockSpec(memory_space=pltpu.VMEM)),
        scratch_shapes=[
            vm((256, 768), BF16), vm((256, 256), F32), vm((1, 128), jnp.int32), pltpu.SMEM((1, 128), jnp.int32),
            vm((1, 1536), jnp.int32), vm((1536, 128), F32), vm((1, 128), F32), vm((ROWS, 256), F32), vm((RUN, 256), F32),
            vm((NH, ROWS, 768), BF16), vm((8, ROWS, 768), BF16), vm((8, ROWS, 256), BF16),
            vm((1536, 384), BF16), vm((8, ROWS, 384), BF16),
            vm((NH, ROWS, 1), F32), vm((NX, 8, 256), F32), vm((NH * ROWS, 1024), BF16),
            vm((8, 8, RUN, 256), F32), vm((8, 8, RUN, 128), F32), vm((8, 8, RUN, 256), F32), vm((8, 8, RUN, 128), F32),
            vm((8, RUN, 256), F32), vm((8, RUN, 128), F32), vm((8, RUN, 256), F32), vm((8, RUN, 128), F32),
            vm((8, 8, RUN, 256), BF16), vm((8, 8, RUN, 128), F32),
            vm((NX, 2, 256, ROWS), F32), vm((NX, 256, ROWS), F32), vm((NX, 256, ROWS), F32), vm((3, 256, ROWS), F32),
            dma((9,)), dma((3, 2)), dma((3, 2)), dma((3, 2)), dma((3, 2)), dma((10,)), dma((10,)), dma((12,)), dma((12,)),
            dma((2, 8)), dma((2, 8)), dma((2, 8)), dma((2, 8)),
            dma((2, 8)), dma((2, 8)), dma((2, 8)), dma((2, 8)), dma((4,)), dma((4,)), dma((6,)), dma((6,)),
            pltpu.SemaphoreType.REGULAR((2,)),
        ],
        compiler_params=pltpu.CompilerParams(collective_id=0, has_side_effects=True, vmem_limit_bytes=67043328),
        name="step",
    )(samples, targets, batch_index, centers, weights, nystrom_index, eigvecs, coefficient)


def solution(mesh):
    in_specs = (
        P("blk", None),
        P("blk", None),
        P("blk"),
        P(("blk", "col"), None),
        P(("blk", "col"), None),
        P(),
        P(),
        P(),
    )
    out_specs = (P(("blk", "col"), None), P(("blk", "col"), None))
    return jax.shard_map(local, mesh=mesh, in_specs=in_specs, out_specs=out_specs, check_vma=False)
```

```python
import jax
import jax.numpy as jnp
from jax import lax
from jax.experimental import pallas as pl
from jax.experimental.pallas import tpu as pltpu
from jax.sharding import PartitionSpec as P

MESH = pl.DeviceIdType.MESH
F32, BF16 = jnp.float32, jnp.bfloat16

shift_sq = 1.0
step_size = 4.0

NX, NY, NZ, NH = 4, 8, 8, 4
RUN = 8
ROWS = 128
STAGE = 9


def spot(x, y, z, core):
    return (x * 8 + (z // 2) * 2 + core, y * 2 + z % 2)


def send(src, dst, sems, where):
    return pltpu.make_async_remote_copy(
        src_ref=src, dst_ref=dst, send_sem=sems[0], recv_sem=sems[1], device_id=where, device_id_type=MESH
    )


def split3(v):
    a = v.astype(BF16)
    rest = v - a.astype(F32)
    b = rest.astype(BF16)
    c = (rest - b.astype(F32)).astype(BF16)
    return a, b, c


def nt(a, b):
    return lax.dot_general(a, b, (((1,), (1,)), ((), ())), preferred_element_type=F32)


def dot(a, b):
    return jnp.dot(a, b, preferred_element_type=F32)


def body(
    samples, targets, index, centers, weights, nys, eig, coef, out,
    samp, targ, idx_v, idx_s, nys_v, eig_v, coef_v, wts, want,
    pts, cen, wlo, e123, ecat, psq, csq, kmat,
    part_py, rec_py, part_pz, rec_pz, part_my, rec_my, part_mz, rec_mz, red_p, red_m, rec2_p, rec2_m, rall, mall, gpart, grec, gs, gx,
    ld, zs, zr, ys, yr, xs, xr, cs, cr, sy, ry, sz, rz, s2, r2, gs1, gr1, gs2, gr2, ds, dr, dxs, dxr, near,
):
    out_res, out_w = out.at[0:RUN], out.at[RUN:RUN + ROWS]
    blk, col = lax.axis_index("blk"), lax.axis_index("col")
    x, h, core = blk // 8, (blk // 2) % 4, blk % 2
    y, low = col // 2, col % 2
    z = 2 * h + low
    other = 1 - core

    def at_y(k):
        return spot(x, (y + k) % NY, z, core)

    def at_z(k):
        return spot(x, y, (z + k) % NZ, core)

    def at_x(k):
        return spot((x + k) % NX, y, z, core)

    partner = spot(x, y, z, other)

    def loop(n, fn, start=0):
        def run(k, carry):
            fn(k)
            return carry

        lax.fori_loop(start, n, run, 0)

    def peers(fn):
        loop(7, lambda i: fn(4 + (i + 1) // 2 * (1 - 2 * (i % 2))))

    barrier = pltpu.get_barrier_semaphore()

    def greet(where):
        pl.semaphore_signal(barrier, inc=1, device_id=where, device_id_type=MESH)

    for where in (at_z(1), at_z(7), at_y(1), at_y(7), at_x(1), at_x(3), partner):
        greet(where)

    mine = 2 * x + core
    loads = [
        pltpu.make_async_copy(index, idx_v.at[0], ld.at[0]),
        pltpu.make_async_copy(samples, samp, ld.at[1]),
        pltpu.make_async_copy(centers, cen.at[mine], ld.at[2]),
        pltpu.make_async_copy(weights, wts, ld.at[3]),
        pltpu.make_async_copy(nys, nys_v.at[0], ld.at[4]),
        pltpu.make_async_copy(eig, eig_v, ld.at[5]),
        pltpu.make_async_copy(coef, coef_v.at[0], ld.at[6]),
        pltpu.make_async_copy(targets, targ, ld.at[7]),
        pltpu.make_async_copy(index, idx_s.at[0], ld.at[8]),
    ]
    for copy in loads:
        copy.start()
    for copy in loads[:2]:
        copy.wait()

    chosen = jnp.where(lax.broadcasted_iota(jnp.int32, (256, ROWS), 0) == idx_v[...], 1.0, 0.0).astype(F32)
    own = dot(chosen.T.astype(BF16), samp[...]).reshape(NY, 2, RUN, 768)
    own = jnp.concatenate([own[:, 0].reshape(64, 768), own[:, 1].reshape(64, 768)], axis=0)
    pts[0] = own.astype(BF16)

    loads[3].wait()
    wlo[mine] = wts[...].astype(BF16)

    pl.semaphore_wait(barrier, 7)
    if STAGE == 0:
        for copy in (loads[2], *loads[4:]):
            copy.wait()
        return

    outward = 2 * low - 1
    zo, zi = spot(x, y, (z + outward + NZ) % NZ, core), spot(x, y, (z - outward + NZ) % NZ, core)
    h_a = ((z + outward + NZ) % NZ) // 2
    h_b = ((z - 2 * outward + NZ) % NZ) // 2
    h_c = ((z + 3 * outward + NZ) % NZ) // 2
    parity = y % 2
    y_to = (at_y(1), at_y(7))

    def zpiece(kind, i, where):
        rows = pl.ds(pl.multiple_of(parity * 64 + i * 32, 32), 32)
        return send(pts.at[kind, rows, :], pts.at[kind + 1, rows, :], (zs.at[kind, i], zr.at[kind, i]), where)

    def ypiece(kind, i, side):
        piece = pts.at[kind + 1, pl.ds(pl.multiple_of(side * 64 + i * 32, 32), 32), :]
        return send(piece, piece, (ys.at[kind, i], yr.at[kind, i]), y_to[i])

    x_next, x_prev, x_far = (x + 1) % NX, (x + 3) % NX, (x + 2) % NX
    right, left = at_x(1), at_x(3)

    def half(block_x, part_no, sem, where):
        piece = cen.at[2 * block_x + core, pl.ds(part_no * 64, 64), :]
        return send(piece, piece, (xs.at[sem], xr.at[sem]), where)

    def weight(block_x, sem, where):
        piece = wlo.at[2 * block_x + core]
        return send(piece, piece, (xs.at[sem], xr.at[sem]), where)

    def weight_half(block_x, part_no, sem, where):
        piece = wlo.at[2 * block_x + core, pl.ds(part_no * 64, 64), :]
        return send(piece, piece, (xs.at[sem], xr.at[sem]), where)

    def across(ref, block_core, block_x, sem):
        piece = ref.at[2 * block_x + block_core]
        return send(piece, piece, (cs.at[sem], cr.at[sem]), partner)

    def hello(no, k):
        for where in (at_y(k), at_y(8 - k)):
            pl.semaphore_signal(near.at[no], inc=1, device_id=where, device_id_type=MESH)

    for i in range(2):
        zpiece(0, i, zo).start()
    hello(0, 1)
    loads[2].wait()
    half(x, 0, 0, right).start()
    half(x, 1, 1, left).start()
    half(x, 1, 2, right).start()
    half(x, 0, 3, left).start()
    across(cen, core, x, 0).start()
    weight(x, 6, right).start()
    weight(x, 7, left).start()
    across(wlo, core, x, 4).start()

    for copy in loads[4:]:
        copy.wait()

    e1, e2, e3 = split3(eig_v[...])
    e123[:, 0:128] = e1
    e123[:, 128:256] = e2
    e123[:, 256:384] = e3

    def eig_rows(xp):
        owner = (xp * 8 + h * 2 + core) * 16 + col
        place = lax.broadcasted_iota(jnp.int32, (ROWS, 1536), 0) + owner * ROWS
        hit = jnp.where(place == nys_v[...], 1.0, 0.0).astype(BF16)
        ecat[2 * xp + core] = dot(hit, e123[...]).astype(BF16)

    def relay_a(i):
        zpiece(0, i, zo).wait_recv()
        zpiece(1, i, zi).start()
        ypiece(0, i, parity).start()

    def relay_b(i):
        zpiece(1, i, zi).wait_recv()
        zpiece(2, i, zo).start()
        ypiece(1, i, parity).start()

    def relay_c(i):
        zpiece(2, i, zo).wait_recv()
        ypiece(2, i, parity).start()

    def points_ready(slot):
        p32 = pts[slot].astype(F32)
        psq[slot] = jnp.sum(p32 * p32, axis=1, keepdims=True)

    def from_y(kind):
        for i in range(2):
            ypiece(kind, i, 1 - parity).wait_recv()
        points_ready(kind + 1)

    def centers_ready(xp):
        for c in range(2):
            v = cen[2 * xp + c].astype(F32)
            total = jnp.sum(v * v, axis=1, keepdims=True)
            csq[xp, :, c * 128:(c + 1) * 128] = jnp.broadcast_to(total, (ROWS, ROWS)).T[0:8, :]

    def pair(xp):
        return pl.ds(pl.multiple_of(xp * 256, 256), 256)

    def unit(slot, end, xp):
        rows = (end - slot) * ROWS
        cross = nt(pts[slot:end].reshape(rows, 768), cen[pl.ds(2 * xp, 2)].reshape(256, 768))
        shifted = psq[slot:end].reshape(rows, 1) + csq[xp, 0:1, :] - 2.0 * cross + shift_sq
        kmat[slot * ROWS:end * ROWS, pair(xp)] = jnp.exp(-(shifted * lax.rsqrt(shifted))).astype(BF16)

    loop(4, eig_rows)
    for i in range(4):
        across(ecat, core, i, 8 + i).start()
    relay_a(0)
    pl.semaphore_wait(near.at[0], 2)
    hello(1, 2)
    relay_a(1)
    half(x_prev, 0, 0, right).wait_recv()
    half(x_prev, 0, 4, right).start()
    half(x_next, 1, 1, left).wait_recv()
    half(x_next, 1, 5, left).start()
    relay_b(0)
    points_ready(0)
    across(cen, other, x, 0).wait_recv()
    centers_ready(x)
    relay_b(1)
    half(x_prev, 1, 2, right).wait_recv()
    across(cen, core, x_prev, 1).start()
    half(x_next, 0, 3, left).wait_recv()
    across(cen, core, x_next, 2).start()
    weight(x_prev, 6, right).wait_recv()
    weight_half(x_prev, 0, 8, right).start()
    across(wlo, core, x_prev, 5).start()
    weight(x_next, 7, left).wait_recv()
    weight_half(x_next, 1, 9, left).start()
    across(wlo, core, x_next, 6).start()
    from_y(0)
    unit(0, 2, x)
    relay_c(0)
    half(x_far, 0, 4, right).wait_recv()
    half(x_far, 1, 5, left).wait_recv()
    across(cen, core, x_far, 3).start()
    across(cen, other, x_prev, 1).wait_recv()
    centers_ready(x_prev)
    across(cen, other, x_next, 2).wait_recv()
    centers_ready(x_next)
    unit(0, 2, x_prev)
    relay_c(1)
    weight_half(x_far, 0, 8, right).wait_recv()
    weight_half(x_far, 1, 9, left).wait_recv()
    across(wlo, core, x_far, 7).start()
    unit(0, 2, x_next)
    from_y(1)
    across(cen, other, x_far, 3).wait_recv()
    centers_ready(x_far)
    unit(0, 2, x_far)
    for i, xp in enumerate((x, x_prev, x_next, x_far)):
        across(wlo, other, xp, 4 + i).wait_recv()
        across(ecat, other, i, 8 + i).wait_recv()
    pl.semaphore_wait(near.at[1], 2)

    slots = (h, h_a, h_b, h_c)
    pred_stream = (part_py, rec_py, part_pz, rec_pz, red_p, rec2_p, 0)
    m_stream = (part_my, rec_my, part_mz, rec_mz, red_m, rec2_m, 1)

    def y_first(stream, g, k):
        no = stream[6]
        return send(stream[0].at[g, (y + k) % NY], stream[1].at[g, k], (sy.at[no, g, k], ry.at[no, g, k]), at_y(k))

    def z_first(stream, k):
        no = stream[6]
        return send(stream[2].at[(z + k) % NZ], stream[3].at[k], (sz.at[no, k], rz.at[no, k]), at_z(k))

    def launch_y(stream, g, value):
        for i in range(2):
            for j in range(2):
                stream[0][g, :, 2 * i + j] = value[i, j]
        peers(lambda k: y_first(stream, g, k).start())

    def launch_z(stream, g, value):
        for i in range(2):
            stream[2][pl.ds(2 * slots[2 * g + i], 2)] = value[i]
        targets = []
        if g == 0:
            targets.append(2 * h + 1 - low)
        else:
            targets += [2 * h_c, 2 * h_c + 1]
        between = h_a if g == 0 else h_b
        targets += [2 * between, 2 * between + 1]
        for target in targets:
            z_first(stream, (target - z + NZ) % NZ).start()

    def group(g):
        k = kmat[256 * g:256 * g + 256, :]
        pred = dot(k, wlo[...].reshape(1024, 256)).reshape(2, 2, 8, RUN, 256)
        m = dot(k, ecat[...].reshape(1024, 384))
        m = (m[:, 0:128] + m[:, 128:256] + m[:, 256:384]).reshape(2, 2, 8, RUN, 128)

        @pl.when(core == 0)
        def _():
            launch_y(pred_stream, g, pred)
            launch_z(m_stream, g, m)

        @pl.when(core == 1)
        def _():
            launch_z(pred_stream, g, pred)
            launch_y(m_stream, g, m)

    group(0)
    from_y(2)
    unit(2, 4, x)
    unit(2, 4, x_prev)
    unit(2, 4, x_next)
    unit(2, 4, x_far)
    group(1)

    def axes(by_z):
        return y + by_z * (z - y), z + by_z * (y - z)

    def by_z(stream):
        return core if stream[6] == 0 else 1 - core

    def second(stream, k):
        flag = by_z(stream)
        no = stream[6]
        where = spot(x, (y + flag * k) % NY, (z + (1 - flag) * k) % NZ, core)
        return send(stream[4].at[(axes(flag)[1] + k) % 8], stream[5].at[k], (s2.at[no, k], r2.at[no, k]), where)

    def finish_first(stream):
        @pl.when(by_z(stream) == 0)
        def _():
            for g in range(2):

                def add(k, total):
                    y_first(stream, g, k).wait_recv()
                    return total + stream[1][g, k]

                total = lax.fori_loop(1, 8, add, stream[0][g, y])
                for i in range(2):
                    stream[4][pl.ds(2 * slots[2 * g + i], 2)] = total[2 * i:2 * i + 2]

        @pl.when(by_z(stream) == 1)
        def _():
            stream[4][...] = stream[2][z]

            def add(k):
                z_first(stream, k).wait_recv()
                stream[4][...] += stream[3][k]

            loop(8, add, 1)

        peers(lambda k: second(stream, k).start())

    def sent_first(stream):
        @pl.when(by_z(stream) == 0)
        def _():
            for g in range(2):
                loop(8, lambda k: y_first(stream, g, k).wait_send(), 1)

        @pl.when(by_z(stream) == 1)
        def _():
            loop(8, lambda k: z_first(stream, k).wait_send(), 1)

    def finish_second(stream):
        def add(k, total):
            second(stream, k).wait_recv()
            return total + stream[5][k]

        return lax.fori_loop(1, 8, add, stream[4][axes(by_z(stream))[1]])

    def r_first(k, src_y):
        return send(rall.at[z, src_y], rall.at[z, src_y], (gs1.at[0, k], gr1.at[0, k]), at_y(k))

    def r_second(k, src_z):
        return send(rall.at[src_z], rall.at[src_z], (gs2.at[0, k], gr2.at[0, k]), at_z(k))

    def m_first(k, src_z):
        return send(mall.at[src_z, y], mall.at[src_z, y], (gs1.at[1, k], gr1.at[1, k]), at_z(k))

    def m_second(k, src_y):
        return send(mall.at[:, src_y], mall.at[:, src_y], (gs2.at[1, k], gr2.at[1, k]), at_y(k))

    def swap(i):
        return send(gpart.at[i, other], grec.at[i], (ds.at[i], dr.at[i]), partner)

    def top(ref):
        return ref.at[0:128]

    def bottom(ref):
        return ref.at[128:256]

    def far_half(i):
        part_of = (top, bottom)[i]
        return send(part_of(gs.at[x_far]), gx.at[2, pl.ds(128 * i, 128)], (dxs.at[i], dxr.at[i]), (right, left)[i])

    def near_half(side, i):
        part_of = (top, bottom)[i]
        block, where = (gs.at[x_next], right) if side == 0 else (gs.at[x_prev], left)
        sem = 2 + 2 * side + i
        return send(part_of(block), gx.at[side, pl.ds(128 * i, 128)], (dxs.at[sem], dxr.at[sem]), where)

    def drain(stage):
        if stage >= 1:
            for i in range(2):
                zpiece(0, i, zo).wait_send()
                zpiece(1, i, zi).wait_send()
                zpiece(2, i, zo).wait_send()
                for kind in range(3):
                    ypiece(kind, i, parity).wait_send()
            for i in range(6):
                half(x, 0, i, right).wait_send()
            for i in range(2):
                weight(x, 6 + i, right).wait_send()
                weight_half(x, 0, 8 + i, right).wait_send()
            for i in range(4):
                across(cen, core, x, i).wait_send()
                across(wlo, core, x, 4 + i).wait_send()
                across(ecat, core, x, 8 + i).wait_send()
        if stage >= 3:
            for stream in (pred_stream, m_stream):
                sent_first(stream)
                loop(8, lambda k: second(stream, k).wait_send(), 1)
        if stage >= 4:
            loop(8, lambda k: r_first(k, y).wait_send(), 1)
            loop(8, lambda k: r_second(k, z).wait_send(), 1)
            loop(8, lambda k: m_first(k, z).wait_send(), 1)
            loop(8, lambda k: m_second(k, y).wait_send(), 1)
        if stage >= 5:
            for i in range(4):
                swap(i).wait_send()
            for i in range(2):
                far_half(i).wait_send()
                near_half(0, i).wait_send()
                near_half(1, i).wait_send()

    for r in range(RUN):
        row = idx_s[0, col * RUN + r]
        want[r:r + 1, :] = targ[pl.ds(row, 1), :]
    finish_first(pred_stream)
    finish_first(m_stream)

    out_res[...] = finish_second(pred_stream) - want[...]
    rall[z, y] = out_res[...].astype(BF16)
    if STAGE == 3:
        finish_second(m_stream)
        return drain(3)

    peers(lambda k: r_first(k, y).start())
    mall[z, y] = finish_second(m_stream)
    peers(lambda k: m_first(k, z).start())
    loop(8, lambda k: r_first(k, (y - k + NY) % NY).wait_recv(), 1)
    peers(lambda k: r_second(k, z).start())
    loop(8, lambda k: m_first(k, (z - k + NZ) % NZ).wait_recv(), 1)
    peers(lambda k: m_second(k, y).start())
    loop(8, lambda k: r_second(k, (z - k + NZ) % NZ).wait_recv(), 1)
    loop(8, lambda k: m_second(k, (y - k + NY) % NY).wait_recv(), 1)
    if STAGE == 4:
        return drain(4)

    resid = jnp.concatenate([rall[pl.ds(2 * t, 2)].astype(F32).reshape(ROWS, 256) for t in slots], axis=0)
    resid_t = resid.T.astype(BF16)
    m_slots = jnp.concatenate([mall[pl.ds(2 * t, 2)].reshape(ROWS, 128) for t in slots], axis=0)
    m1, m2, m3 = split3(m_slots)
    proj = dot(resid_t, m1) + dot(resid_t, m2) + dot(resid_t, m3)
    a1, a2, a3 = split3(proj * coef_v[...])
    a_one = jnp.concatenate([a1, a1, a1], axis=1)
    a_two = jnp.concatenate([a2, a2], axis=1)

    def grad(xp):
        e = ecat[pl.ds(2 * xp, 2)].reshape(256, 384)
        g = dot(resid_t, kmat[:, pair(xp)])
        g = g - (nt(a_one, e) + nt(a_two, e[:, 0:256]) + nt(a3, e[:, 0:128]))
        gpart[xp, 0] = g[:, 0:128]
        gpart[xp, 1] = g[:, 128:256]
        swap(xp).start()

    def summed(xp):
        swap(xp).wait_recv()
        gs[xp] = gpart[xp, core] + grec[xp]

    grad(x_far)
    grad(x_next)
    summed(x_far)
    far_half(0).start()
    far_half(1).start()
    grad(x_prev)
    summed(x_next)
    near_half(0, 1).start()
    grad(x)
    summed(x_prev)
    near_half(1, 0).start()
    far_half(0).wait_recv()
    gs[x_next, 0:128, :] += gx[2, 0:128, :]
    near_half(0, 0).start()
    far_half(1).wait_recv()
    gs[x_prev, 128:256, :] += gx[2, 128:256, :]
    near_half(1, 1).start()
    summed(x)
    near_half(0, 1).wait_recv()
    near_half(1, 0).wait_recv()
    near_half(0, 0).wait_recv()
    near_half(1, 1).wait_recv()
    total = gs[x] + gx[0] + gx[1]
    out_w[...] = wts[...] - step_size * total.T
    drain(5)


def local(samples, targets, batch_index, centers, weights, nystrom_index, eigvecs, coefficient):
    dma = pltpu.SemaphoreType.DMA
    vm = pltpu.VMEM
    out = pl.pallas_call(
        body,
        out_shape=jax.ShapeDtypeStruct((RUN + ROWS, 256), F32),
        in_specs=[pl.BlockSpec(memory_space=pl.ANY)] * 8,
        out_specs=pl.BlockSpec(memory_space=pltpu.VMEM),
        scratch_shapes=[
            vm((256, 768), BF16), vm((256, 256), F32), vm((1, 128), jnp.int32), pltpu.SMEM((1, 128), jnp.int32),
            vm((1, 1536), jnp.int32), vm((1536, 128), F32), vm((1, 128), F32), vm((ROWS, 256), F32), vm((RUN, 256), F32),
            vm((NH, ROWS, 768), BF16), vm((8, ROWS, 768), BF16), vm((8, ROWS, 256), BF16),
            vm((1536, 384), BF16), vm((8, ROWS, 384), BF16),
            vm((NH, ROWS, 1), F32), vm((NX, 8, 256), F32), vm((NH * ROWS, 1024), BF16),
            vm((2, 8, 4, RUN, 256), F32), vm((2, 8, 4, RUN, 256), F32), vm((8, 8, RUN, 256), F32), vm((8, 8, RUN, 256), F32),
            vm((2, 8, 4, RUN, 128), F32), vm((2, 8, 4, RUN, 128), F32), vm((8, 8, RUN, 128), F32), vm((8, 8, RUN, 128), F32),
            vm((8, RUN, 256), F32), vm((8, RUN, 128), F32), vm((8, RUN, 256), F32), vm((8, RUN, 128), F32),
            vm((8, 8, RUN, 256), BF16), vm((8, 8, RUN, 128), F32),
            vm((NX, 2, 256, ROWS), F32), vm((NX, 256, ROWS), F32), vm((NX, 256, ROWS), F32), vm((3, 256, ROWS), F32),
            dma((9,)), dma((3, 2)), dma((3, 2)), dma((3, 2)), dma((3, 2)), dma((10,)), dma((10,)), dma((12,)), dma((12,)),
            dma((2, 2, 8)), dma((2, 2, 8)), dma((2, 8)), dma((2, 8)), dma((2, 8)), dma((2, 8)),
            dma((2, 8)), dma((2, 8)), dma((2, 8)), dma((2, 8)), dma((4,)), dma((4,)), dma((6,)), dma((6,)),
            pltpu.SemaphoreType.REGULAR((2,)),
        ],
        compiler_params=pltpu.CompilerParams(collective_id=0, has_side_effects=True, vmem_limit_bytes=67043328),
        name="step",
    )(samples, targets, batch_index, centers, weights, nystrom_index, eigvecs, coefficient)
    return out[0:RUN], out[RUN:]


def solution(mesh):
    in_specs = (
        P("blk", None),
        P("blk", None),
        P("blk"),
        P(("blk", "col"), None),
        P(("blk", "col"), None),
        P(),
        P(),
        P(),
    )
    out_specs = (P(("blk", "col"), None), P(("blk", "col"), None))
    return jax.shard_map(local, mesh=mesh, in_specs=in_specs, out_specs=out_specs, check_vma=False)
```

```python
import jax
import jax.numpy as jnp
from jax import lax
from jax.experimental import pallas as pl
from jax.experimental.pallas import tpu as pltpu
from jax.sharding import PartitionSpec as P

MESH = pl.DeviceIdType.MESH
F32, BF16 = jnp.float32, jnp.bfloat16

shift_sq = 1.0
step_size = 4.0

NX, NY, NZ, NH = 4, 8, 8, 4
RUN = 8
ROWS = 128
STAGE = 9


def spot(x, y, z, core):
    return (x * 8 + (z // 2) * 2 + core, y * 2 + z % 2)


def send(src, dst, sems, where):
    return pltpu.make_async_remote_copy(
        src_ref=src, dst_ref=dst, send_sem=sems[0], recv_sem=sems[1], device_id=where, device_id_type=MESH
    )


def split3(v):
    a = v.astype(BF16)
    rest = v - a.astype(F32)
    b = rest.astype(BF16)
    c = (rest - b.astype(F32)).astype(BF16)
    return a, b, c


def nt(a, b):
    return lax.dot_general(a, b, (((1,), (1,)), ((), ())), preferred_element_type=F32)


def dot(a, b):
    return jnp.dot(a, b, preferred_element_type=F32)


def body(
    samples, targets, index, centers, weights, nys, eig, coef, out,
    samp, targ, idx_v, idx_s, nys_v, eig_v, coef_v, wts, want,
    pts, cen, wlo, e123, ecat, psq, csq, kmat,
    part_py, rec_py, part_pz, rec_pz, part_my, rec_my, part_mz, rec_mz, red_p, red_m, rec2_p, rec2_m, rall, mall, gpart, grec, gs, gx,
    ld, zs, zr, ys, yr, xs, xr, cs, cr, sy, ry, sz, rz, s2, r2, gs1, gr1, gs2, gr2, ds, dr, dxs, dxr, near,
):
    out_res, out_w = out.at[0:RUN], out.at[RUN:RUN + ROWS]
    blk, col = lax.axis_index("blk"), lax.axis_index("col")
    x, h, core = blk // 8, (blk // 2) % 4, blk % 2
    y, low = col // 2, col % 2
    z = 2 * h + low
    other = 1 - core

    def at_y(k):
        return spot(x, (y + k) % NY, z, core)

    def at_z(k):
        return spot(x, y, (z + k) % NZ, core)

    def at_x(k):
        return spot((x + k) % NX, y, z, core)

    partner = spot(x, y, z, other)

    def loop(n, fn, start=0):
        def run(k, carry):
            fn(k)
            return carry

        lax.fori_loop(start, n, run, 0)

    def peers(fn):
        loop(7, lambda i: fn(4 + (i + 1) // 2 * (1 - 2 * (i % 2))))

    barrier = pltpu.get_barrier_semaphore()

    def greet(where):
        pl.semaphore_signal(barrier, inc=1, device_id=where, device_id_type=MESH)

    for where in (at_z(1), at_z(7), at_y(1), at_y(7), at_x(1), at_x(3), partner):
        greet(where)

    mine = 2 * x + core
    loads = [
        pltpu.make_async_copy(index, idx_v.at[0], ld.at[0]),
        pltpu.make_async_copy(samples, samp, ld.at[1]),
        pltpu.make_async_copy(centers, cen.at[mine], ld.at[2]),
        pltpu.make_async_copy(weights, wts, ld.at[3]),
        pltpu.make_async_copy(nys, nys_v.at[0], ld.at[4]),
        pltpu.make_async_copy(eig, eig_v, ld.at[5]),
        pltpu.make_async_copy(coef, coef_v.at[0], ld.at[6]),
        pltpu.make_async_copy(targets, targ, ld.at[7]),
        pltpu.make_async_copy(index, idx_s.at[0], ld.at[8]),
    ]
    for copy in loads:
        copy.start()
    for copy in loads[:2]:
        copy.wait()

    chosen = jnp.where(lax.broadcasted_iota(jnp.int32, (256, ROWS), 0) == idx_v[...], 1.0, 0.0).astype(F32)
    own = dot(chosen.T.astype(BF16), samp[...]).reshape(NY, 2, RUN, 768)
    own = jnp.concatenate([own[:, 0].reshape(64, 768), own[:, 1].reshape(64, 768)], axis=0)
    pts[2] = own.astype(BF16)

    loads[3].wait()
    wlo[mine] = wts[...].astype(BF16)

    pl.semaphore_wait(barrier, 7)
    if STAGE == 0:
        for copy in (loads[2], *loads[4:]):
            copy.wait()
        return

    outward = 2 * low - 1
    zo, zi = spot(x, y, (z + outward + NZ) % NZ, core), spot(x, y, (z - outward + NZ) % NZ, core)
    h_a = ((z + outward + NZ) % NZ) // 2
    h_b = ((z - 2 * outward + NZ) % NZ) // 2
    h_c = ((z + 3 * outward + NZ) % NZ) // 2
    parity = y % 2
    y_to = (at_y(1), at_y(7))

    held_in, lands_in = (2, 0, 1), (0, 1, 3)

    def zpiece(kind, i, where):
        rows = pl.ds(pl.multiple_of(parity * 64 + i * 32, 32), 32)
        return send(pts.at[held_in[kind], rows, :], pts.at[lands_in[kind], rows, :], (zs.at[kind, i], zr.at[kind, i]), where)

    def ypiece(kind, i, side):
        piece = pts.at[lands_in[kind], pl.ds(pl.multiple_of(side * 64 + i * 32, 32), 32), :]
        return send(piece, piece, (ys.at[kind, i], yr.at[kind, i]), y_to[i])

    x_next, x_prev, x_far = (x + 1) % NX, (x + 3) % NX, (x + 2) % NX
    right, left = at_x(1), at_x(3)

    def half(block_x, part_no, sem, where):
        piece = cen.at[2 * block_x + core, pl.ds(part_no * 64, 64), :]
        return send(piece, piece, (xs.at[sem], xr.at[sem]), where)

    def weight(block_x, sem, where):
        piece = wlo.at[2 * block_x + core]
        return send(piece, piece, (xs.at[sem], xr.at[sem]), where)

    def weight_half(block_x, part_no, sem, where):
        piece = wlo.at[2 * block_x + core, pl.ds(part_no * 64, 64), :]
        return send(piece, piece, (xs.at[sem], xr.at[sem]), where)

    def across(ref, block_core, block_x, sem):
        piece = ref.at[2 * block_x + block_core]
        return send(piece, piece, (cs.at[sem], cr.at[sem]), partner)

    def hello(no, k):
        for where in (at_y(k), at_y(8 - k)):
            pl.semaphore_signal(near.at[no], inc=1, device_id=where, device_id_type=MESH)

    for i in range(2):
        zpiece(0, i, zo).start()
    hello(0, 1)
    loads[2].wait()
    half(x, 0, 0, right).start()
    half(x, 1, 1, left).start()
    half(x, 1, 2, right).start()
    half(x, 0, 3, left).start()
    across(cen, core, x, 0).start()
    weight(x, 6, right).start()
    weight(x, 7, left).start()
    across(wlo, core, x, 4).start()

    for copy in loads[4:]:
        copy.wait()

    e1, e2, e3 = split3(eig_v[...])
    e123[:, 0:128] = e1
    e123[:, 128:256] = e2
    e123[:, 256:384] = e3

    def eig_rows(xp):
        owner = (xp * 8 + h * 2 + core) * 16 + col
        place = lax.broadcasted_iota(jnp.int32, (ROWS, 1536), 0) + owner * ROWS
        hit = jnp.where(place == nys_v[...], 1.0, 0.0).astype(BF16)
        ecat[2 * xp + core] = dot(hit, e123[...]).astype(BF16)

    def relay_a(i):
        zpiece(0, i, zo).wait_recv()
        zpiece(1, i, zi).start()
        ypiece(0, i, parity).start()

    def relay_b(i):
        zpiece(1, i, zi).wait_recv()
        zpiece(2, i, zo).start()
        ypiece(1, i, parity).start()

    def relay_c(i):
        zpiece(2, i, zo).wait_recv()
        ypiece(2, i, parity).start()

    def points_ready(slot):
        p32 = pts[slot].astype(F32)
        psq[slot] = jnp.sum(p32 * p32, axis=1, keepdims=True)

    def from_y(kind):
        for i in range(2):
            ypiece(kind, i, 1 - parity).wait_recv()
        points_ready(lands_in[kind])

    def centers_ready(xp):
        for c in range(2):
            v = cen[2 * xp + c].astype(F32)
            total = jnp.sum(v * v, axis=1, keepdims=True)
            csq[xp, :, c * 128:(c + 1) * 128] = jnp.broadcast_to(total, (ROWS, ROWS)).T[0:8, :]

    def pair(xp):
        return pl.ds(pl.multiple_of(xp * 256, 256), 256)

    def unit(slot, end, xp):
        rows = (end - slot) * ROWS
        cross = nt(pts[slot:end].reshape(rows, 768), cen[pl.ds(2 * xp, 2)].reshape(256, 768))
        shifted = psq[slot:end].reshape(rows, 1) + csq[xp, 0:1, :] - 2.0 * cross + shift_sq
        kmat[slot * ROWS:end * ROWS, pair(xp)] = jnp.exp(-(shifted * lax.rsqrt(shifted))).astype(BF16)

    loop(4, eig_rows)
    for i in range(4):
        across(ecat, core, i, 8 + i).start()
    relay_a(0)
    pl.semaphore_wait(near.at[0], 2)
    hello(1, 2)
    relay_a(1)
    half(x_prev, 0, 0, right).wait_recv()
    half(x_prev, 0, 4, right).start()
    half(x_next, 1, 1, left).wait_recv()
    half(x_next, 1, 5, left).start()
    relay_b(0)
    points_ready(2)
    across(cen, other, x, 0).wait_recv()
    centers_ready(x)
    relay_b(1)
    half(x_prev, 1, 2, right).wait_recv()
    across(cen, core, x_prev, 1).start()
    half(x_next, 0, 3, left).wait_recv()
    across(cen, core, x_next, 2).start()
    weight(x_prev, 6, right).wait_recv()
    weight_half(x_prev, 0, 8, right).start()
    across(wlo, core, x_prev, 5).start()
    weight(x_next, 7, left).wait_recv()
    weight_half(x_next, 1, 9, left).start()
    across(wlo, core, x_next, 6).start()
    from_y(0)
    half(x_far, 0, 4, right).wait_recv()
    half(x_far, 1, 5, left).wait_recv()
    across(cen, core, x_far, 3).start()
    relay_c(0)
    across(cen, other, x_prev, 1).wait_recv()
    centers_ready(x_prev)
    across(cen, other, x_next, 2).wait_recv()
    centers_ready(x_next)
    relay_c(1)
    from_y(1)
    unit(0, 2, x)
    weight_half(x_far, 0, 8, right).wait_recv()
    weight_half(x_far, 1, 9, left).wait_recv()
    across(wlo, core, x_far, 7).start()
    unit(0, 2, x_prev)
    unit(0, 2, x_next)
    across(cen, other, x_far, 3).wait_recv()
    centers_ready(x_far)
    unit(0, 2, x_far)
    for i, xp in enumerate((x, x_prev, x_next, x_far)):
        across(wlo, other, xp, 4 + i).wait_recv()
        across(ecat, other, i, 8 + i).wait_recv()
    pl.semaphore_wait(near.at[1], 2)

    slots = (h_a, h_b, h, h_c)
    pred_stream = (part_py, rec_py, part_pz, rec_pz, red_p, rec2_p, 0)
    m_stream = (part_my, rec_my, part_mz, rec_mz, red_m, rec2_m, 1)

    def y_first(stream, g, k):
        no = stream[6]
        return send(stream[0].at[g, (y + k) % NY], stream[1].at[g, k], (sy.at[no, g, k], ry.at[no, g, k]), at_y(k))

    def z_first(stream, k):
        no = stream[6]
        return send(stream[2].at[(z + k) % NZ], stream[3].at[k], (sz.at[no, k], rz.at[no, k]), at_z(k))

    def launch_y(stream, g, value):
        for i in range(2):
            for j in range(2):
                stream[0][g, :, 2 * i + j] = value[i, j]
        peers(lambda k: y_first(stream, g, k).start())

    def launch_z(stream, g, value):
        for i in range(2):
            stream[2][pl.ds(2 * slots[2 * g + i], 2)] = value[i]
        if g == 0:
            targets = (2 * h_b, 2 * h_b + 1, 2 * h_a, 2 * h_a + 1)
        else:
            targets = (2 * h_c, 2 * h_c + 1, 2 * h + 1 - low)
        for target in targets:
            z_first(stream, (target - z + NZ) % NZ).start()

    def group(g):
        k = kmat[256 * g:256 * g + 256, :]
        pred = dot(k, wlo[...].reshape(1024, 256)).reshape(2, 2, 8, RUN, 256)
        m = dot(k, ecat[...].reshape(1024, 384))
        m = (m[:, 0:128] + m[:, 128:256] + m[:, 256:384]).reshape(2, 2, 8, RUN, 128)

        @pl.when(core == 0)
        def _():
            launch_y(pred_stream, g, pred)
            launch_z(m_stream, g, m)

        @pl.when(core == 1)
        def _():
            launch_z(pred_stream, g, pred)
            launch_y(m_stream, g, m)

    group(0)
    from_y(2)
    unit(2, 4, x)
    unit(2, 4, x_prev)
    unit(2, 4, x_next)
    unit(2, 4, x_far)
    group(1)

    def axes(by_z):
        return y + by_z * (z - y), z + by_z * (y - z)

    def by_z(stream):
        return core if stream[6] == 0 else 1 - core

    def second(stream, k):
        flag = by_z(stream)
        no = stream[6]
        where = spot(x, (y + flag * k) % NY, (z + (1 - flag) * k) % NZ, core)
        return send(stream[4].at[(axes(flag)[1] + k) % 8], stream[5].at[k], (s2.at[no, k], r2.at[no, k]), where)

    def finish_first(stream):
        @pl.when(by_z(stream) == 0)
        def _():
            for g in range(2):

                def add(k, total):
                    y_first(stream, g, k).wait_recv()
                    return total + stream[1][g, k]

                total = lax.fori_loop(1, 8, add, stream[0][g, y])
                for i in range(2):
                    stream[4][pl.ds(2 * slots[2 * g + i], 2)] = total[2 * i:2 * i + 2]

        @pl.when(by_z(stream) == 1)
        def _():
            stream[4][...] = stream[2][z]

            def add(k):
                z_first(stream, k).wait_recv()
                stream[4][...] += stream[3][k]

            loop(8, add, 1)

        peers(lambda k: second(stream, k).start())

    def sent_first(stream):
        @pl.when(by_z(stream) == 0)
        def _():
            for g in range(2):
                loop(8, lambda k: y_first(stream, g, k).wait_send(), 1)

        @pl.when(by_z(stream) == 1)
        def _():
            loop(8, lambda k: z_first(stream, k).wait_send(), 1)

    def finish_second(stream):
        def add(k, total):
            second(stream, k).wait_recv()
            return total + stream[5][k]

        return lax.fori_loop(1, 8, add, stream[4][axes(by_z(stream))[1]])

    def r_first(k, src_y):
        return send(rall.at[z, src_y], rall.at[z, src_y], (gs1.at[0, k], gr1.at[0, k]), at_y(k))

    def r_second(k, src_z):
        return send(rall.at[src_z], rall.at[src_z], (gs2.at[0, k], gr2.at[0, k]), at_z(k))

    def m_first(k, src_z):
        return send(mall.at[src_z, y], mall.at[src_z, y], (gs1.at[1, k], gr1.at[1, k]), at_z(k))

    def m_second(k, src_y):
        return send(mall.at[:, src_y], mall.at[:, src_y], (gs2.at[1, k], gr2.at[1, k]), at_y(k))

    def swap(i):
        return send(gpart.at[i, other], grec.at[i], (ds.at[i], dr.at[i]), partner)

    def top(ref):
        return ref.at[0:128]

    def bottom(ref):
        return ref.at[128:256]

    def far_half(i):
        part_of = (top, bottom)[i]
        return send(part_of(gs.at[x_far]), gx.at[2, pl.ds(128 * i, 128)], (dxs.at[i], dxr.at[i]), (right, left)[i])

    def near_half(side, i):
        part_of = (top, bottom)[i]
        block, where = (gs.at[x_next], right) if side == 0 else (gs.at[x_prev], left)
        sem = 2 + 2 * side + i
        return send(part_of(block), gx.at[side, pl.ds(128 * i, 128)], (dxs.at[sem], dxr.at[sem]), where)

    def drain(stage):
        if stage >= 1:
            for i in range(2):
                zpiece(0, i, zo).wait_send()
                zpiece(1, i, zi).wait_send()
                zpiece(2, i, zo).wait_send()
                for kind in range(3):
                    ypiece(kind, i, parity).wait_send()
            for i in range(6):
                half(x, 0, i, right).wait_send()
            for i in range(2):
                weight(x, 6 + i, right).wait_send()
                weight_half(x, 0, 8 + i, right).wait_send()
            for i in range(4):
                across(cen, core, x, i).wait_send()
                across(wlo, core, x, 4 + i).wait_send()
                across(ecat, core, x, 8 + i).wait_send()
        if stage >= 3:
            for stream in (pred_stream, m_stream):
                sent_first(stream)
                loop(8, lambda k: second(stream, k).wait_send(), 1)
        if stage >= 4:
            loop(8, lambda k: r_first(k, y).wait_send(), 1)
            loop(8, lambda k: r_second(k, z).wait_send(), 1)
            loop(8, lambda k: m_first(k, z).wait_send(), 1)
            loop(8, lambda k: m_second(k, y).wait_send(), 1)
        if stage >= 5:
            for i in range(4):
                swap(i).wait_send()
            for i in range(2):
                far_half(i).wait_send()
                near_half(0, i).wait_send()
                near_half(1, i).wait_send()

    for r in range(RUN):
        row = idx_s[0, col * RUN + r]
        want[r:r + 1, :] = targ[pl.ds(row, 1), :]
    finish_first(pred_stream)
    finish_first(m_stream)

    out_res[...] = finish_second(pred_stream) - want[...]
    rall[z, y] = out_res[...].astype(BF16)
    if STAGE == 3:
        finish_second(m_stream)
        return drain(3)

    peers(lambda k: r_first(k, y).start())
    mall[z, y] = finish_second(m_stream)
    peers(lambda k: m_first(k, z).start())
    loop(8, lambda k: r_first(k, (y - k + NY) % NY).wait_recv(), 1)
    peers(lambda k: r_second(k, z).start())
    loop(8, lambda k: m_first(k, (z - k + NZ) % NZ).wait_recv(), 1)
    peers(lambda k: m_second(k, y).start())
    loop(8, lambda k: r_second(k, (z - k + NZ) % NZ).wait_recv(), 1)
    loop(8, lambda k: m_second(k, (y - k + NY) % NY).wait_recv(), 1)
    if STAGE == 4:
        return drain(4)

    resid = jnp.concatenate([rall[pl.ds(2 * t, 2)].astype(F32).reshape(ROWS, 256) for t in slots], axis=0)
    resid_t = resid.T.astype(BF16)
    m_slots = jnp.concatenate([mall[pl.ds(2 * t, 2)].reshape(ROWS, 128) for t in slots], axis=0)
    m1, m2, m3 = split3(m_slots)
    proj = dot(resid_t, m1) + dot(resid_t, m2) + dot(resid_t, m3)
    a1, a2, a3 = split3(proj * coef_v[...])
    a_one = jnp.concatenate([a1, a1, a1], axis=1)
    a_two = jnp.concatenate([a2, a2], axis=1)

    def grad(xp):
        e = ecat[pl.ds(2 * xp, 2)].reshape(256, 384)
        g = dot(resid_t, kmat[:, pair(xp)])
        g = g - (nt(a_one, e) + nt(a_two, e[:, 0:256]) + nt(a3, e[:, 0:128]))
        gpart[xp, 0] = g[:, 0:128]
        gpart[xp, 1] = g[:, 128:256]
        swap(xp).start()

    def summed(xp):
        swap(xp).wait_recv()
        gs[xp] = gpart[xp, core] + grec[xp]

    grad(x_far)
    summed(x_far)
    far_half(0).start()
    far_half(1).start()
    grad(x_next)
    grad(x_prev)
    summed(x_next)
    near_half(0, 1).start()
    grad(x)
    summed(x_prev)
    near_half(1, 0).start()
    far_half(0).wait_recv()
    gs[x_next, 0:128, :] += gx[2, 0:128, :]
    near_half(0, 0).start()
    far_half(1).wait_recv()
    gs[x_prev, 128:256, :] += gx[2, 128:256, :]
    near_half(1, 1).start()
    summed(x)
    near_half(0, 1).wait_recv()
    near_half(1, 0).wait_recv()
    near_half(0, 0).wait_recv()
    near_half(1, 1).wait_recv()
    total = gs[x] + gx[0] + gx[1]
    out_w[...] = wts[...] - step_size * total.T
    drain(5)


def local(samples, targets, batch_index, centers, weights, nystrom_index, eigvecs, coefficient):
    dma = pltpu.SemaphoreType.DMA
    vm = pltpu.VMEM
    out = pl.pallas_call(
        body,
        out_shape=jax.ShapeDtypeStruct((RUN + ROWS, 256), F32),
        in_specs=[pl.BlockSpec(memory_space=pl.ANY)] * 8,
        out_specs=pl.BlockSpec(memory_space=pltpu.VMEM),
        scratch_shapes=[
            vm((256, 768), BF16), vm((256, 256), F32), vm((1, 128), jnp.int32), pltpu.SMEM((1, 128), jnp.int32),
            vm((1, 1536), jnp.int32), vm((1536, 128), F32), vm((1, 128), F32), vm((ROWS, 256), F32), vm((RUN, 256), F32),
            vm((NH, ROWS, 768), BF16), vm((8, ROWS, 768), BF16), vm((8, ROWS, 256), BF16),
            vm((1536, 384), BF16), vm((8, ROWS, 384), BF16),
            vm((NH, ROWS, 1), F32), vm((NX, 8, 256), F32), vm((NH * ROWS, 1024), BF16),
            vm((2, 8, 4, RUN, 256), F32), vm((2, 8, 4, RUN, 256), F32), vm((8, 8, RUN, 256), F32), vm((8, 8, RUN, 256), F32),
            vm((2, 8, 4, RUN, 128), F32), vm((2, 8, 4, RUN, 128), F32), vm((8, 8, RUN, 128), F32), vm((8, 8, RUN, 128), F32),
            vm((8, RUN, 256), F32), vm((8, RUN, 128), F32), vm((8, RUN, 256), F32), vm((8, RUN, 128), F32),
            vm((8, 8, RUN, 256), BF16), vm((8, 8, RUN, 128), F32),
            vm((NX, 2, 256, ROWS), F32), vm((NX, 256, ROWS), F32), vm((NX, 256, ROWS), F32), vm((3, 256, ROWS), F32),
            dma((9,)), dma((3, 2)), dma((3, 2)), dma((3, 2)), dma((3, 2)), dma((10,)), dma((10,)), dma((12,)), dma((12,)),
            dma((2, 2, 8)), dma((2, 2, 8)), dma((2, 8)), dma((2, 8)), dma((2, 8)), dma((2, 8)),
            dma((2, 8)), dma((2, 8)), dma((2, 8)), dma((2, 8)), dma((4,)), dma((4,)), dma((6,)), dma((6,)),
            pltpu.SemaphoreType.REGULAR((2,)),
        ],
        compiler_params=pltpu.CompilerParams(collective_id=0, has_side_effects=True, vmem_limit_bytes=67043328),
        name="step",
    )(samples, targets, batch_index, centers, weights, nystrom_index, eigvecs, coefficient)
    return out[0:RUN], out[RUN:]


def solution(mesh):
    in_specs = (
        P("blk", None),
        P("blk", None),
        P("blk"),
        P(("blk", "col"), None),
        P(("blk", "col"), None),
        P(),
        P(),
        P(),
    )
    out_specs = (P(("blk", "col"), None), P(("blk", "col"), None))
    return jax.shard_map(local, mesh=mesh, in_specs=in_specs, out_specs=out_specs, check_vma=False)
```

```python
import jax
import jax.numpy as jnp
from jax import lax
from jax.experimental import pallas as pl
from jax.experimental.pallas import tpu as pltpu
from jax.sharding import PartitionSpec as P

MESH = pl.DeviceIdType.MESH
F32, BF16 = jnp.float32, jnp.bfloat16

shift_sq = 1.0
step_size = 4.0

NX, NY, NZ, NH = 4, 8, 8, 4
RUN = 8
ROWS = 128
STAGE = 9


def spot(x, y, z, core):
    return (x * 8 + (z // 2) * 2 + core, y * 2 + z % 2)


def send(src, dst, sems, where):
    return pltpu.make_async_remote_copy(
        src_ref=src, dst_ref=dst, send_sem=sems[0], recv_sem=sems[1], device_id=where, device_id_type=MESH
    )


def split3(v):
    a = v.astype(BF16)
    rest = v - a.astype(F32)
    b = rest.astype(BF16)
    c = (rest - b.astype(F32)).astype(BF16)
    return a, b, c


def nt(a, b):
    return lax.dot_general(a, b, (((1,), (1,)), ((), ())), preferred_element_type=F32)


def dot(a, b):
    return jnp.dot(a, b, preferred_element_type=F32)


def body(
    samples, targets, index, centers, weights, nys, eig, coef, out,
    samp, targ, idx_v, idx_s, nys_v, eig_v, coef_v, wts, want,
    pts, cen, wlo, e123, ecat, psq, csq, kmat,
    part_py, rec_py, part_pz, rec_pz, part_my, rec_my, part_mz, rec_mz, red_p, red_m, rec2_p, rec2_m, rall, mall, gpart, grec, gs, gx,
    ld, zs, zr, ys, yr, xs, xr, cs, cr, sy, ry, sz, rz, s2, r2, gs1, gr1, gs2, gr2, ds, dr, dxs, dxr, near,
):
    out_res, out_w = out.at[0:RUN], out.at[RUN:RUN + ROWS]
    blk, col = lax.axis_index("blk"), lax.axis_index("col")
    x, h, core = blk // 8, (blk // 2) % 4, blk % 2
    y, low = col // 2, col % 2
    z = 2 * h + low
    other = 1 - core

    def at_y(k):
        return spot(x, (y + k) % NY, z, core)

    def at_z(k):
        return spot(x, y, (z + k) % NZ, core)

    def at_x(k):
        return spot((x + k) % NX, y, z, core)

    partner = spot(x, y, z, other)

    def loop(n, fn, start=0):
        def run(k, carry):
            fn(k)
            return carry

        lax.fori_loop(start, n, run, 0)

    def peers(fn):
        loop(7, lambda i: fn(4 + (i + 1) // 2 * (1 - 2 * (i % 2))))

    barrier = pltpu.get_barrier_semaphore()

    def greet(where):
        pl.semaphore_signal(barrier, inc=1, device_id=where, device_id_type=MESH)

    for where in (at_z(1), at_z(7), at_y(1), at_y(7), at_x(1), at_x(3), partner):
        greet(where)

    mine = 2 * x + core
    loads = [
        pltpu.make_async_copy(index, idx_v.at[0], ld.at[0]),
        pltpu.make_async_copy(samples, samp, ld.at[1]),
        pltpu.make_async_copy(centers, cen.at[mine], ld.at[2]),
        pltpu.make_async_copy(weights, wts, ld.at[3]),
        pltpu.make_async_copy(nys, nys_v.at[0], ld.at[4]),
        pltpu.make_async_copy(eig, eig_v, ld.at[5]),
        pltpu.make_async_copy(coef, coef_v.at[0], ld.at[6]),
        pltpu.make_async_copy(targets, targ, ld.at[7]),
        pltpu.make_async_copy(index, idx_s.at[0], ld.at[8]),
    ]
    for copy in loads:
        copy.start()
    for copy in loads[:2]:
        copy.wait()

    chosen = jnp.where(lax.broadcasted_iota(jnp.int32, (256, ROWS), 0) == idx_v[...], 1.0, 0.0).astype(F32)
    own = dot(chosen.T.astype(BF16), samp[...]).reshape(NY, 2, RUN, 768)
    own = jnp.concatenate([own[:, 0].reshape(64, 768), own[:, 1].reshape(64, 768)], axis=0)
    pts[2] = own.astype(BF16)

    loads[3].wait()
    wlo[mine] = wts[...].astype(BF16)

    pl.semaphore_wait(barrier, 7)
    if STAGE == 0:
        for copy in (loads[2], *loads[4:]):
            copy.wait()
        return

    outward = 2 * low - 1
    zo, zi = spot(x, y, (z + outward + NZ) % NZ, core), spot(x, y, (z - outward + NZ) % NZ, core)
    h_a = ((z + outward + NZ) % NZ) // 2
    h_b = ((z - 2 * outward + NZ) % NZ) // 2
    h_c = ((z + 3 * outward + NZ) % NZ) // 2
    parity = y % 2
    y_to = (at_y(1), at_y(7))

    held_in, lands_in = (2, 0, 1), (0, 1, 3)

    def zpiece(kind, i, where):
        rows = pl.ds(pl.multiple_of(parity * 64 + i * 32, 32), 32)
        return send(pts.at[held_in[kind], rows, :], pts.at[lands_in[kind], rows, :], (zs.at[kind, i], zr.at[kind, i]), where)

    def ypiece(kind, i, side):
        piece = pts.at[lands_in[kind], pl.ds(pl.multiple_of(side * 64 + i * 32, 32), 32), :]
        return send(piece, piece, (ys.at[kind, i], yr.at[kind, i]), y_to[i])

    x_next, x_prev, x_far = (x + 1) % NX, (x + 3) % NX, (x + 2) % NX
    right, left = at_x(1), at_x(3)

    def half(block_x, part_no, sem, where):
        piece = cen.at[2 * block_x + core, pl.ds(part_no * 64, 64), :]
        return send(piece, piece, (xs.at[sem], xr.at[sem]), where)

    def weight(block_x, sem, where):
        piece = wlo.at[2 * block_x + core]
        return send(piece, piece, (xs.at[sem], xr.at[sem]), where)

    def weight_half(block_x, part_no, sem, where):
        piece = wlo.at[2 * block_x + core, pl.ds(part_no * 64, 64), :]
        return send(piece, piece, (xs.at[sem], xr.at[sem]), where)

    def across(ref, block_core, block_x, sem):
        piece = ref.at[2 * block_x + block_core]
        return send(piece, piece, (cs.at[sem], cr.at[sem]), partner)

    def hello(no, k):
        for where in (at_y(k), at_y(8 - k)):
            pl.semaphore_signal(near.at[no], inc=1, device_id=where, device_id_type=MESH)

    for i in range(2):
        zpiece(0, i, zo).start()
    hello(0, 1)
    loads[2].wait()
    half(x, 0, 0, right).start()
    half(x, 1, 1, left).start()
    half(x, 1, 2, right).start()
    half(x, 0, 3, left).start()
    across(cen, core, x, 0).start()
    weight(x, 6, right).start()
    weight(x, 7, left).start()
    across(wlo, core, x, 4).start()

    for copy in loads[4:]:
        copy.wait()

    e1, e2, e3 = split3(eig_v[...])
    e123[:, 0:128] = e1
    e123[:, 128:256] = e2
    e123[:, 256:384] = e3

    def eig_rows(xp):
        owner = (xp * 8 + h * 2 + core) * 16 + col
        place = lax.broadcasted_iota(jnp.int32, (ROWS, 1536), 0) + owner * ROWS
        hit = jnp.where(place == nys_v[...], 1.0, 0.0).astype(BF16)
        ecat[2 * xp + core] = dot(hit, e123[...]).astype(BF16)

    def relay_a(i):
        zpiece(0, i, zo).wait_recv()
        zpiece(1, i, zi).start()
        ypiece(0, i, parity).start()

    def relay_b(i):
        zpiece(1, i, zi).wait_recv()
        zpiece(2, i, zo).start()
        ypiece(1, i, parity).start()

    def relay_c(i):
        zpiece(2, i, zo).wait_recv()
        ypiece(2, i, parity).start()

    def points_ready(slot):
        p32 = pts[slot].astype(F32)
        psq[slot] = jnp.sum(p32 * p32, axis=1, keepdims=True)

    def from_y(kind):
        for i in range(2):
            ypiece(kind, i, 1 - parity).wait_recv()
        points_ready(lands_in[kind])

    def centers_ready(xp):
        for c in range(2):
            v = cen[2 * xp + c].astype(F32)
            total = jnp.sum(v * v, axis=1, keepdims=True)
            csq[xp, :, c * 128:(c + 1) * 128] = jnp.broadcast_to(total, (ROWS, ROWS)).T[0:8, :]

    def pair(xp):
        return pl.ds(pl.multiple_of(xp * 256, 256), 256)

    def unit(slot, end, xp):
        rows = (end - slot) * ROWS
        cross = nt(pts[slot:end].reshape(rows, 768), cen[pl.ds(2 * xp, 2)].reshape(256, 768))
        shifted = psq[slot:end].reshape(rows, 1) + csq[xp, 0:1, :] - 2.0 * cross + shift_sq
        kmat[slot * ROWS:end * ROWS, pair(xp)] = jnp.exp(-(shifted * lax.rsqrt(shifted))).astype(BF16)

    loop(4, eig_rows)
    for i in range(4):
        across(ecat, core, i, 8 + i).start()
    relay_a(0)
    pl.semaphore_wait(near.at[0], 2)
    hello(1, 2)
    relay_a(1)
    half(x_prev, 0, 0, right).wait_recv()
    half(x_prev, 0, 4, right).start()
    half(x_next, 1, 1, left).wait_recv()
    half(x_next, 1, 5, left).start()
    relay_b(0)
    points_ready(2)
    across(cen, other, x, 0).wait_recv()
    centers_ready(x)
    relay_b(1)
    half(x_prev, 1, 2, right).wait_recv()
    across(cen, core, x_prev, 1).start()
    half(x_next, 0, 3, left).wait_recv()
    across(cen, core, x_next, 2).start()
    weight(x_prev, 6, right).wait_recv()
    weight_half(x_prev, 0, 8, right).start()
    across(wlo, core, x_prev, 5).start()
    weight(x_next, 7, left).wait_recv()
    weight_half(x_next, 1, 9, left).start()
    across(wlo, core, x_next, 6).start()
    from_y(0)
    half(x_far, 0, 4, right).wait_recv()
    half(x_far, 1, 5, left).wait_recv()
    across(cen, core, x_far, 3).start()
    relay_c(0)
    across(cen, other, x_prev, 1).wait_recv()
    centers_ready(x_prev)
    across(cen, other, x_next, 2).wait_recv()
    centers_ready(x_next)
    relay_c(1)
    from_y(1)
    unit(0, 2, x)
    weight_half(x_far, 0, 8, right).wait_recv()
    weight_half(x_far, 1, 9, left).wait_recv()
    across(wlo, core, x_far, 7).start()
    unit(0, 2, x_prev)
    unit(0, 2, x_next)
    across(cen, other, x_far, 3).wait_recv()
    centers_ready(x_far)
    unit(0, 2, x_far)
    for i, xp in enumerate((x, x_prev, x_next, x_far)):
        across(wlo, other, xp, 4 + i).wait_recv()
        across(ecat, other, i, 8 + i).wait_recv()
    pl.semaphore_wait(near.at[1], 2)

    slots = (h_a, h_b, h, h_c)
    pred_stream = (part_py, rec_py, part_pz, rec_pz, red_p, rec2_p, 0)
    m_stream = (part_my, rec_my, part_mz, rec_mz, red_m, rec2_m, 1)

    def y_first(stream, g, k):
        no = stream[6]
        return send(stream[0].at[g, (y + k) % NY], stream[1].at[g, k], (sy.at[no, g, k], ry.at[no, g, k]), at_y(k))

    def z_first(stream, k):
        no = stream[6]
        return send(stream[2].at[(z + k) % NZ], stream[3].at[k], (sz.at[no, k], rz.at[no, k]), at_z(k))

    def launch_y(stream, g, value):
        for i in range(2):
            for j in range(2):
                stream[0][g, :, 2 * i + j] = value[i, j]
        peers(lambda k: y_first(stream, g, k).start())

    def launch_z(stream, g, value):
        for i in range(2):
            stream[2][pl.ds(2 * slots[2 * g + i], 2)] = value[i]
        if g == 0:
            targets = (2 * h_b, 2 * h_b + 1, 2 * h_a, 2 * h_a + 1)
        else:
            targets = (2 * h_c, 2 * h_c + 1, 2 * h + 1 - low)
        for target in targets:
            z_first(stream, (target - z + NZ) % NZ).start()

    def group(g):
        k = kmat[256 * g:256 * g + 256, :]
        pred = dot(k, wlo[...].reshape(1024, 256)).reshape(2, 2, 8, RUN, 256)
        m = dot(k, ecat[...].reshape(1024, 384))
        m = (m[:, 0:128] + m[:, 128:256] + m[:, 256:384]).reshape(2, 2, 8, RUN, 128)

        @pl.when(core == 0)
        def _():
            launch_y(pred_stream, g, pred)
            launch_z(m_stream, g, m)

        @pl.when(core == 1)
        def _():
            launch_z(pred_stream, g, pred)
            launch_y(m_stream, g, m)

    group(0)
    from_y(2)
    unit(2, 4, x)
    unit(2, 4, x_prev)
    unit(2, 4, x_next)
    unit(2, 4, x_far)
    group(1)

    def axes(by_z):
        return y + by_z * (z - y), z + by_z * (y - z)

    def by_z(stream):
        return core if stream[6] == 0 else 1 - core

    def second(stream, k):
        flag = by_z(stream)
        no = stream[6]
        where = spot(x, (y + flag * k) % NY, (z + (1 - flag) * k) % NZ, core)
        return send(stream[4].at[(axes(flag)[1] + k) % 8], stream[5].at[k], (s2.at[no, k], r2.at[no, k]), where)

    def finish_first(stream):
        @pl.when(by_z(stream) == 0)
        def _():
            for g in range(2):

                def add(k, total):
                    y_first(stream, g, k).wait_recv()
                    return total + stream[1][g, k]

                total = lax.fori_loop(1, 8, add, stream[0][g, y])
                for i in range(2):
                    stream[4][pl.ds(2 * slots[2 * g + i], 2)] = total[2 * i:2 * i + 2]

        @pl.when(by_z(stream) == 1)
        def _():
            stream[4][...] = stream[2][z]

            def add(k):
                z_first(stream, k).wait_recv()
                stream[4][...] += stream[3][k]

            loop(8, add, 1)

        peers(lambda k: second(stream, k).start())

    def sent_first(stream):
        @pl.when(by_z(stream) == 0)
        def _():
            for g in range(2):
                loop(8, lambda k: y_first(stream, g, k).wait_send(), 1)

        @pl.when(by_z(stream) == 1)
        def _():
            loop(8, lambda k: z_first(stream, k).wait_send(), 1)

    def finish_second(stream):
        def add(k, total):
            second(stream, k).wait_recv()
            return total + stream[5][k]

        return lax.fori_loop(1, 8, add, stream[4][axes(by_z(stream))[1]])

    def r_first(k, src_y):
        return send(rall.at[z, src_y], rall.at[z, src_y], (gs1.at[0, k], gr1.at[0, k]), at_y(k))

    def r_second(k, src_z):
        return send(rall.at[src_z], rall.at[src_z], (gs2.at[0, k], gr2.at[0, k]), at_z(k))

    def m_first(k, src_z):
        return send(mall.at[src_z, y], mall.at[src_z, y], (gs1.at[1, k], gr1.at[1, k]), at_z(k))

    def m_second(k, src_y):
        return send(mall.at[:, src_y], mall.at[:, src_y], (gs2.at[1, k], gr2.at[1, k]), at_y(k))

    def swap(i):
        return send(gpart.at[i, other], grec.at[i], (ds.at[i], dr.at[i]), partner)

    def top(ref):
        return ref.at[0:128]

    def bottom(ref):
        return ref.at[128:256]

    def far_half(i):
        part_of = (top, bottom)[i]
        return send(part_of(gs.at[x_far]), gx.at[2, pl.ds(128 * i, 128)], (dxs.at[i], dxr.at[i]), (right, left)[i])

    def near_half(side, i):
        part_of = (top, bottom)[i]
        block, where = (gs.at[x_next], right) if side == 0 else (gs.at[x_prev], left)
        sem = 2 + 2 * side + i
        return send(part_of(block), gx.at[side, pl.ds(128 * i, 128)], (dxs.at[sem], dxr.at[sem]), where)

    def drain(stage):
        if stage >= 1:
            for i in range(2):
                zpiece(0, i, zo).wait_send()
                zpiece(1, i, zi).wait_send()
                zpiece(2, i, zo).wait_send()
                for kind in range(3):
                    ypiece(kind, i, parity).wait_send()
            for i in range(6):
                half(x, 0, i, right).wait_send()
            for i in range(2):
                weight(x, 6 + i, right).wait_send()
                weight_half(x, 0, 8 + i, right).wait_send()
            for i in range(4):
                across(cen, core, x, i).wait_send()
                across(wlo, core, x, 4 + i).wait_send()
                across(ecat, core, x, 8 + i).wait_send()
        if stage >= 3:
            for stream in (pred_stream, m_stream):
                sent_first(stream)
                loop(8, lambda k: second(stream, k).wait_send(), 1)
        if stage >= 4:
            loop(8, lambda k: r_first(k, y).wait_send(), 1)
            loop(8, lambda k: r_second(k, z).wait_send(), 1)
            loop(8, lambda k: m_first(k, z).wait_send(), 1)
            loop(8, lambda k: m_second(k, y).wait_send(), 1)
        if stage >= 5:
            for i in range(4):
                swap(i).wait_send()
            for i in range(2):
                far_half(i).wait_send()
                near_half(0, i).wait_send()
                near_half(1, i).wait_send()

    for r in range(RUN):
        row = idx_s[0, col * RUN + r]
        want[r:r + 1, :] = targ[pl.ds(row, 1), :]
    finish_first(pred_stream)
    finish_first(m_stream)

    out_res[...] = finish_second(pred_stream) - want[...]
    rall[z, y] = out_res[...].astype(BF16)
    if STAGE == 3:
        finish_second(m_stream)
        return drain(3)

    peers(lambda k: r_first(k, y).start())
    mall[z, y] = finish_second(m_stream)
    peers(lambda k: m_first(k, z).start())
    loop(8, lambda k: r_first(k, (y - k + NY) % NY).wait_recv(), 1)
    peers(lambda k: r_second(k, z).start())
    loop(8, lambda k: m_first(k, (z - k + NZ) % NZ).wait_recv(), 1)
    peers(lambda k: m_second(k, y).start())
    loop(8, lambda k: r_second(k, (z - k + NZ) % NZ).wait_recv(), 1)

    resid = jnp.concatenate([rall[pl.ds(2 * t, 2)].astype(F32).reshape(ROWS, 256) for t in slots], axis=0)
    resid_t = resid.T.astype(BF16)
    loop(8, lambda k: m_second(k, (y - k + NY) % NY).wait_recv(), 1)
    m_slots = jnp.concatenate([mall[pl.ds(2 * t, 2)].reshape(ROWS, 128) for t in slots], axis=0)
    m1, m2, m3 = split3(m_slots)
    proj = dot(resid_t, m1) + dot(resid_t, m2) + dot(resid_t, m3)
    a1, a2, a3 = split3(proj * coef_v[...])
    a_one = jnp.concatenate([a1, a1, a1], axis=1)
    a_two = jnp.concatenate([a2, a2], axis=1)

    def grad(xp):
        e = ecat[pl.ds(2 * xp, 2)].reshape(256, 384)
        g = dot(resid_t, kmat[:, pair(xp)])
        g = g - (nt(a_one, e) + nt(a_two, e[:, 0:256]) + nt(a3, e[:, 0:128]))
        gpart[xp, 0] = g[:, 0:128]
        gpart[xp, 1] = g[:, 128:256]
        swap(xp).start()

    def summed(xp):
        swap(xp).wait_recv()
        gs[xp] = gpart[xp, core] + grec[xp]

    grad(x_far)
    summed(x_far)
    far_half(0).start()
    far_half(1).start()
    grad(x_next)
    grad(x_prev)
    summed(x_next)
    near_half(0, 1).start()
    summed(x_prev)
    near_half(1, 0).start()
    grad(x)
    far_half(0).wait_recv()
    gs[x_next, 0:128, :] += gx[2, 0:128, :]
    near_half(0, 0).start()
    far_half(1).wait_recv()
    gs[x_prev, 128:256, :] += gx[2, 128:256, :]
    near_half(1, 1).start()
    summed(x)
    near_half(0, 1).wait_recv()
    near_half(1, 0).wait_recv()
    near_half(0, 0).wait_recv()
    near_half(1, 1).wait_recv()
    total = gs[x] + gx[0] + gx[1]
    out_w[...] = wts[...] - step_size * total.T
    drain(5)


def local(samples, targets, batch_index, centers, weights, nystrom_index, eigvecs, coefficient):
    dma = pltpu.SemaphoreType.DMA
    vm = pltpu.VMEM
    out = pl.pallas_call(
        body,
        out_shape=jax.ShapeDtypeStruct((RUN + ROWS, 256), F32),
        in_specs=[pl.BlockSpec(memory_space=pl.ANY)] * 8,
        out_specs=pl.BlockSpec(memory_space=pltpu.VMEM),
        scratch_shapes=[
            vm((256, 768), BF16), vm((256, 256), F32), vm((1, 128), jnp.int32), pltpu.SMEM((1, 128), jnp.int32),
            vm((1, 1536), jnp.int32), vm((1536, 128), F32), vm((1, 128), F32), vm((ROWS, 256), F32), vm((RUN, 256), F32),
            vm((NH, ROWS, 768), BF16), vm((8, ROWS, 768), BF16), vm((8, ROWS, 256), BF16),
            vm((1536, 384), BF16), vm((8, ROWS, 384), BF16),
            vm((NH, ROWS, 1), F32), vm((NX, 8, 256), F32), vm((NH * ROWS, 1024), BF16),
            vm((2, 8, 4, RUN, 256), F32), vm((2, 8, 4, RUN, 256), F32), vm((8, 8, RUN, 256), F32), vm((8, 8, RUN, 256), F32),
            vm((2, 8, 4, RUN, 128), F32), vm((2, 8, 4, RUN, 128), F32), vm((8, 8, RUN, 128), F32), vm((8, 8, RUN, 128), F32),
            vm((8, RUN, 256), F32), vm((8, RUN, 128), F32), vm((8, RUN, 256), F32), vm((8, RUN, 128), F32),
            vm((8, 8, RUN, 256), BF16), vm((8, 8, RUN, 128), F32),
            vm((NX, 2, 256, ROWS), F32), vm((NX, 256, ROWS), F32), vm((NX, 256, ROWS), F32), vm((3, 256, ROWS), F32),
            dma((9,)), dma((3, 2)), dma((3, 2)), dma((3, 2)), dma((3, 2)), dma((10,)), dma((10,)), dma((12,)), dma((12,)),
            dma((2, 2, 8)), dma((2, 2, 8)), dma((2, 8)), dma((2, 8)), dma((2, 8)), dma((2, 8)),
            dma((2, 8)), dma((2, 8)), dma((2, 8)), dma((2, 8)), dma((4,)), dma((4,)), dma((6,)), dma((6,)),
            pltpu.SemaphoreType.REGULAR((2,)),
        ],
        compiler_params=pltpu.CompilerParams(collective_id=0, has_side_effects=True, vmem_limit_bytes=67043328),
        name="step",
    )(samples, targets, batch_index, centers, weights, nystrom_index, eigvecs, coefficient)
    return out[0:RUN], out[RUN:]


def solution(mesh):
    in_specs = (
        P("blk", None),
        P("blk", None),
        P("blk"),
        P(("blk", "col"), None),
        P(("blk", "col"), None),
        P(),
        P(),
        P(),
    )
    out_specs = (P(("blk", "col"), None), P(("blk", "col"), None))
    return jax.shard_map(local, mesh=mesh, in_specs=in_specs, out_specs=out_specs, check_vma=False)
```
